256 devices in a mesh: ctx: 64 (over z, x, core), kvh: 4 (over y).
Axes of the slice: x: 4, y: 4, z: 8, core: 2. Of those that a mesh axis runs over, the one named last changes fastest.
Arguments:
- query_rows: bfloat16 [16384, 4096], P('ctx', 'kvh'), may hold values from -6 to 6
- key_rows: bfloat16 [16384, 1024], P('ctx', 'kvh'), may hold values from -6 to 6
- value_rows: bfloat16 [16384, 1024], P('ctx', 'kvh'), may hold values from -60 to 60
- grad_out: bfloat16 [16384, 4096], P('ctx', 'kvh'), may hold values from -6 to 6
- chosen: int32 [32, 2], replicated, may hold values from 0 to 31, as said below
Outputs:
- normed: bfloat16 [16384, 4096], P('ctx', 'kvh')
- grad_query: bfloat16 [16384, 4096], P('ctx', 'kvh')
- grad_key: bfloat16 [16384, 1024], P('ctx', 'kvh')
- grad_value: bfloat16 [16384, 1024], P('ctx', 'kvh')
The draws below stay inside these ranges and needn't reach their ends.
Inputs may be any that keep to these rules, and one draw needn't show every extreme that they name: For query block b with b >= 2, chosen[b, 0] and chosen[b, 1] are distinct and below b. chosen[1, 0] = 0. Slots of blocks 0 and 1 that have no earlier block hold 31.
All inputs are finite; a program needn't handle non-finite values.
Results may differ from the reference program's by a relative error of at most 0.013.
Values may be sent and summed in bfloat16 or wider, within the bound.
A program may use at most 128 MiB of HBM per device.

```python
import math
import jax
import jax.numpy as jnp
from jax import lax

HEADS = 32
KV_HEADS = 8
HEAD_DIM = 128
BLOCK = 512
BLOCKS = 32
SEQ = 16384


def draw_query_rows(key, part):
    own_key = jax.random.fold_in(key, 1)
    base = jnp.clip(jax.random.normal(own_key, (SEQ, HEADS, HEAD_DIM)), -6.0, 6.0)
    return base.astype(jnp.float32).reshape(SEQ, HEADS * HEAD_DIM).astype(jnp.bfloat16)


def draw_key_rows(key, part):
    own_key = jax.random.fold_in(key, 2)
    base = jnp.clip(jax.random.normal(own_key, (SEQ, KV_HEADS, HEAD_DIM)), -6.0, 6.0)
    return base.astype(jnp.float32).reshape(SEQ, KV_HEADS * HEAD_DIM).astype(jnp.bfloat16)


def draw_value_rows(key, part):
    own_key = jax.random.fold_in(key, 5)
    head_scale = 10.0 ** (jnp.arange(KV_HEADS, dtype=jnp.float32) / (KV_HEADS - 1))
    base = jnp.clip(jax.random.normal(own_key, (SEQ, KV_HEADS, HEAD_DIM)), -6.0, 6.0)
    scaled = base * head_scale[None, :, None]
    return scaled.astype(jnp.float32).reshape(SEQ, KV_HEADS * HEAD_DIM).astype(jnp.bfloat16)


def draw_chosen(key, part):
    blocks = jnp.arange(BLOCKS, dtype=jnp.int32)
    span = jnp.maximum(blocks, 1)
    early = jax.random.randint(jax.random.fold_in(key, 3), (BLOCKS,), 0, span)
    first = jnp.where(span >= 8, early * early // span, early)
    span_two = jnp.maximum(blocks - 1, 1)
    other = jax.random.randint(jax.random.fold_in(key, 4), (BLOCKS,), 0, span_two)
    second = jnp.where(span_two >= 8, other * other // span_two, other)
    second = jnp.where(second >= first, second + 1, second)
    last_block = BLOCKS - 1
    first = jnp.where(blocks >= 1, first, last_block)
    second = jnp.where(blocks >= 2, second, last_block)
    return jnp.stack([first, second], axis=1).astype(jnp.int32)


def steps_of(stream_key, shape, shards, low, high):
    gain, own = 1.0, jax.random.fold_in(stream_key, 6)
    for axis_at, blocks in shards:
        draws = jnp.exp(jax.random.uniform(jax.random.fold_in(own, axis_at), (blocks,), jnp.float32, low / len(shards), high / len(shards)))
        gain = gain * jnp.repeat(draws, shape[axis_at] // blocks).reshape([-1 if axis == axis_at else 1 for axis in range(len(shape))])
    return gain


def centred(key, dims, width, reach, pieces=(), held_as=jnp.bfloat16):
    array = jax.random.normal(key, dims, jnp.float32) * width
    if len(pieces) > 0:
        array = steps_of(key, dims, pieces, -0.22, 0.18) * array
    return jnp.clip(array, min=-reach, max=reach).astype(held_as)


def setup_inputs(seed: int = 0) -> dict:
    keys = jax.random.split(jax.random.key(seed), 6)
    query_rows = draw_query_rows(jax.random.fold_in(keys[5], 71), 0)
    key_rows = draw_key_rows(jax.random.fold_in(keys[5], 71), 0)
    value_rows = draw_value_rows(jax.random.fold_in(keys[5], 71), 0)
    grad_out = centred(keys[3], (SEQ, HEADS * HEAD_DIM), 1.0, 6.0, ((0, 64), (1, 4)))
    chosen = draw_chosen(jax.random.fold_in(keys[5], 71), 0)
    return {"query_rows": query_rows, "key_rows": key_rows, "value_rows": value_rows, "grad_out": grad_out, "chosen": chosen}


def block_order(offsets):
    half = BLOCK // 2
    return 2 * (offsets % half) + offsets % BLOCK // half

def visible_mask(picks, index):
    places = jnp.arange(3 * BLOCK, dtype=jnp.int32)
    section = places // BLOCK
    allowed = (section == 0) | (section == 1) & (picks[0] < index) | (section == 2) & (picks[1] < index)
    causal = block_order(places)[None, :] <= block_order(jnp.arange(BLOCK, dtype=jnp.int32))[:, None]
    return allowed[None, :] & ((section[None, :] > 0) | causal)

def gathered(blocks, picks, index):
    own = blocks[index]
    return jnp.concatenate([own, blocks[picks[0]], blocks[picks[1]]], axis=0).astype(jnp.float32)

def probabilities(queries, keys_all, visible):
    scale = 1.0 / math.sqrt(HEAD_DIM)
    scores = jnp.einsum('qgrd,kgd->grqk', queries, keys_all) * scale
    scores = jnp.where(visible[None, None], scores, -jnp.inf)
    top = lax.optimization_barrier(jnp.max(scores, axis=-1, keepdims=True))
    weights = jnp.exp(scores - top)
    return weights / lax.optimization_barrier(jnp.sum(weights, axis=-1, keepdims=True))

def rounded_copy(values):
    return lax.optimization_barrier(values.astype(jnp.bfloat16)).astype(jnp.float32)

def reference(query_rows, key_rows, value_rows, grad_out, chosen):
    group = HEADS // KV_HEADS
    scale = 1.0 / math.sqrt(HEAD_DIM)
    key_blocks = key_rows.reshape(BLOCKS, BLOCK, KV_HEADS, HEAD_DIM)
    value_blocks = value_rows.reshape(BLOCKS, BLOCK, KV_HEADS, HEAD_DIM)
    query_blocks = query_rows.reshape(BLOCKS, BLOCK, KV_HEADS, group, HEAD_DIM)
    indices = jnp.arange(BLOCKS, dtype=jnp.int32)

    def forward(index):
        picks = chosen[index]
        keys_all = gathered(key_blocks, picks, index)
        values_all = gathered(value_blocks, picks, index)
        queries = query_blocks[index].astype(jnp.float32)
        probs = probabilities(queries, keys_all, visible_mask(picks, index))
        output = jnp.einsum('grqk,kgd->qgrd', rounded_copy(probs), values_all)
        return output.reshape(BLOCK, HEADS * HEAD_DIM).astype(jnp.bfloat16)
    attended = lax.map(forward, indices).reshape(SEQ, HEADS * HEAD_DIM)
    wide = attended.astype(jnp.float32)
    upstream = grad_out.astype(jnp.float32)
    meansq = lax.optimization_barrier(jnp.mean(wide * wide, axis=1, keepdims=True))
    cross = lax.optimization_barrier(jnp.mean(upstream * wide, axis=1, keepdims=True))
    rscale = lax.rsqrt(meansq + 1e-06)
    normed = (wide * rscale).astype(jnp.bfloat16)
    grad_att = (rscale * upstream - wide * (rscale ** 3 * cross)).astype(jnp.bfloat16)
    grad_blocks = grad_att.reshape(BLOCKS, BLOCK, KV_HEADS, group, HEAD_DIM)

    def backward(carry, index):
        key_total, value_total = carry
        picks = chosen[index]
        keys_all = gathered(key_blocks, picks, index)
        values_all = gathered(value_blocks, picks, index)
        queries = query_blocks[index].astype(jnp.float32)
        probs = probabilities(queries, keys_all, visible_mask(picks, index))
        probs_round = rounded_copy(probs)
        upstream_block = grad_blocks[index].astype(jnp.float32)
        dprob = jnp.einsum('qgrd,kgd->grqk', upstream_block, values_all)
        delta = lax.optimization_barrier(jnp.sum(probs * dprob, axis=-1, keepdims=True))
        dscore = rounded_copy(probs * (dprob - delta) * scale)
        query_grad = jnp.einsum('grqk,kgd->qgrd', dscore, keys_all).reshape(BLOCK, HEADS * HEAD_DIM).astype(jnp.bfloat16)
        key_part = jnp.einsum('grqk,qgrd->kgd', dscore, queries)
        value_part = jnp.einsum('grqk,qgrd->kgd', probs_round, upstream_block)
        key_total = key_total.at[index].add(key_part[:BLOCK])
        value_total = value_total.at[index].add(value_part[:BLOCK])
        for slot in range(2):
            weight = (picks[slot] < index).astype(jnp.float32)
            key_total = key_total.at[picks[slot]].add(weight * key_part[(slot + 1) * BLOCK:(slot + 2) * BLOCK])
            value_total = value_total.at[picks[slot]].add(weight * value_part[(slot + 1) * BLOCK:(slot + 2) * BLOCK])
        return ((key_total, value_total), query_grad)
    start = jnp.zeros((BLOCKS, BLOCK, KV_HEADS, HEAD_DIM), jnp.float32)
    (key_total, value_total), query_grads = lax.scan(backward, (start, start), indices)
    grad_query = query_grads.reshape(SEQ, HEADS * HEAD_DIM)
    grad_key = key_total.reshape(SEQ, KV_HEADS * HEAD_DIM).astype(jnp.bfloat16)
    grad_value = value_total.reshape(SEQ, KV_HEADS * HEAD_DIM).astype(jnp.bfloat16)
    return (normed, grad_query, grad_key, grad_value)
```

```python
import functools
import math

import jax
import jax.numpy as jnp
from jax import lax
from jax.experimental import pallas as pl
from jax.experimental.pallas import tpu as pltpu
from jax.sharding import PartitionSpec as P

HEADS = 32
HEAD_DIM = 128
EPSILON = 1e-06
SCALE = 1.0 / math.sqrt(HEAD_DIM)
SCALE2 = SCALE * math.log2(math.e)
MESH = pl.DeviceIdType.MESH
F32 = jnp.float32
BF16 = jnp.bfloat16
NEG = -jnp.inf


def dot(left, right):
    return jnp.dot(left, right, preferred_element_type=F32)


def aligned(start, size, step):
    return pl.ds(pl.multiple_of(start, step), size)


def kernel(
    blocks, rows, group, kvh,
    chosen, q_in, k_in, v_in, g_in,
    normed_out, gq_out, gk_out, gv_out,
    qs, gos, kv, vtx, kt, qt, gt, held, picked, probs, maxes, parts, weights, att_wide,
    stat_send, stat_recv, gat, ga, delta, dqt, dkv, dkv_send, arrived, table, totals, home,
    nrm, gq, gkv,
    local_sem, swap_send, swap_recv, hop_send, hop_recv, stat_sems, out_local, out_send, out_recv,
):
    hd = HEAD_DIM
    block = 2 * rows
    piece = block // blocks
    width = group * hd
    ctx = lax.axis_index("ctx")
    y = lax.axis_index("kvh")
    mine = ctx // 2
    core = lax.rem(ctx, 2)
    other = 1 - core
    partner = (2 * mine + other, y)
    members = 2 * kvh
    slot = 2 * y + core

    def peer(step):
        return lax.rem(mine + step, blocks)

    def member(step):
        at = lax.rem(slot + step, members)
        return (2 * mine + lax.rem(at, 2), at // 2)

    def drain(ref, sem):
        pltpu.make_async_copy(ref, ref, sem).wait()

    def send(src, dst, send_sem, recv_sem, device):
        pltpu.make_async_remote_copy(
            src_ref=src, dst_ref=dst, send_sem=send_sem, recv_sem=recv_sem,
            device_id=device, device_id_type=MESH,
        ).start()

    own_rows = aligned(core * rows, rows, rows)
    other_rows = aligned(other * rows, rows, rows)
    own_head = aligned(core * hd, hd, hd)
    other_head = aligned(other * hd, hd, hd)
    own_group = aligned(core * width, width, width)
    other_group = aligned(other * width, width, width)
    k_lanes = pl.ds(0, hd)
    v_lanes = pl.ds(hd, hd)

    fetches = [
        pltpu.make_async_copy(k_in.at[:, own_head], kv.at[own_rows, k_lanes], local_sem.at[0]),
        pltpu.make_async_copy(v_in.at[:, own_head], kv.at[own_rows, v_lanes], local_sem.at[1]),
        pltpu.make_async_copy(q_in.at[:, own_group], qs.at[own_rows, :], local_sem.at[2]),
        pltpu.make_async_copy(g_in.at[:, own_group], gos.at[own_rows, :], local_sem.at[3]),
    ]
    for fetch in fetches:
        fetch.start()

    barrier = pltpu.get_barrier_semaphore()

    @pl.loop(1, blocks)
    def _(step):
        pl.semaphore_signal(
            barrier, inc=1, device_id=(2 * peer(step) + core, y), device_id_type=MESH
        )

    @pl.loop(1, members)
    def _(step):
        pl.semaphore_signal(barrier, inc=1, device_id=member(step), device_id_type=MESH)

    pl.semaphore_wait(barrier, blocks + members - 2)

    swaps = [
        (k_in.at[:, other_head], kv.at[own_rows, k_lanes]),
        (v_in.at[:, other_head], kv.at[own_rows, v_lanes]),
        (q_in.at[:, other_group], qs.at[own_rows, :]),
        (g_in.at[:, other_group], gos.at[own_rows, :]),
    ]
    for number, (src, dst) in enumerate(swaps):
        send(src, dst, swap_send.at[number], swap_recv.at[number], partner)
    fetches[0].wait()
    fetches[1].wait()

    def scatter_half(half):
        count = blocks // 2

        @pl.loop(0, count)
        def _(step):
            to = half * count + lax.rem(step + mine, count)

            @pl.when(to != mine)
            def _():
                send(
                    kv.at[aligned(piece * to, piece, piece), :], held.at[mine],
                    hop_send.at[0], hop_recv.at[0], (2 * to + core, y),
                )

    scatter_half(core)
    drain(kv.at[other_rows, k_lanes], swap_recv.at[0])
    drain(kv.at[other_rows, v_lanes], swap_recv.at[1])
    scatter_half(other)
    held[mine] = kv[aligned(piece * mine, piece, piece), :]

    fetches[2].wait()
    fetches[3].wait()
    drain(qs.at[other_rows, :], swap_recv.at[2])
    drain(gos.at[other_rows, :], swap_recv.at[3])

    def turn_keys(section):
        at = pl.ds(section * block, block)
        kt[section] = kv[at, 0:hd].T
        vtx[section, 0:hd, :] = kv[at, hd : 2 * hd].T
        vtx[section, hd : hd + 16, :] = jnp.ones((16, block), BF16)

    def forward(section, head):
        keys = kv[section * block : (section + 1) * block, 0:hd]
        scores = dot(keys, qt[head])
        if section == 0:
            key_at = lax.broadcasted_iota(jnp.int32, (block, block), 0)
            row_at = lax.broadcasted_iota(jnp.int32, (block, block), 1)
            key_order = 2 * lax.rem(key_at, rows) + key_at // rows
            row_order = 2 * lax.rem(row_at, rows) + row_at // rows
            scores = jnp.where(key_order <= row_order, scores, NEG)
        top = jnp.max(scores, axis=0, keepdims=True)
        terms = jnp.exp2((scores - top) * SCALE2).astype(BF16)
        probs[section, head] = terms
        maxes[section, head] = jnp.broadcast_to(top, (8, block))
        parts[section, head] = dot(vtx[section], terms)

    turn_keys(0)

    @pl.loop(0, group)
    def _(head):
        lanes = aligned(head * hd, hd, hd)
        qt[head] = qs[:, lanes].T
        gt[head] = gos[:, lanes].T

    for pick in range(2):
        lane_owner = lax.broadcasted_iota(jnp.int32, (8, block), 1) // piece

        def fill(reader, owners):
            choice = chosen[reader, pick]
            choice = jnp.where(choice < reader, choice, -1)
            return jnp.where(lane_owner == reader, choice, owners)

        owners = lax.fori_loop(0, blocks, fill, jnp.full((8, block), -1, jnp.int32))
        row_at = lax.broadcasted_iota(jnp.int32, (block, block), 0)
        lane_at = lax.broadcasted_iota(jnp.int32, (block, block), 1)
        wanted = owners[0:1] * piece + lax.rem(lane_at, piece)
        table[pick] = (row_at == wanted).astype(F32).astype(BF16)

    forward(0, 0)

    drain(held.at[pl.ds(0, blocks - 1)], hop_recv.at[0])
    for pick in range(2):
        base = (1 + pick) * block

        @pl.loop(1, blocks)
        def _(step):
            to = peer(step)
            picked[pick, to] = held[chosen[to, pick]]
            send(
                picked.at[pick, to], kv.at[aligned(base + piece * mine, piece, piece), :],
                hop_send.at[1 + pick], hop_recv.at[1 + pick], (2 * to + core, y),
            )

        kv[aligned(base + piece * mine, piece, piece), :] = held[chosen[mine, pick]]

    @pl.loop(1, group)
    def _(head):
        forward(0, head)

    for pick in range(2):
        base = (1 + pick) * block
        drain(kv.at[pl.ds(base, block - piece), :], hop_recv.at[1 + pick])
        turn_keys(1 + pick)

        @pl.loop(0, group)
        def _(head):
            forward(1 + pick, head)

    valid = [chosen[mine, pick] < mine for pick in range(2)]

    def merge(head, sums):
        top_own = maxes[0, head, 0:1]
        tops = [top_own] + [
            jnp.where(valid[pick], maxes[1 + pick, head, 0:1], NEG) for pick in range(2)
        ]
        top = jnp.maximum(jnp.maximum(tops[0], tops[1]), tops[2])
        ratios = [jnp.exp2((value - top) * SCALE2) for value in tops]
        total = sum(
            ratio * parts[section, head, hd : hd + 1] for section, ratio in enumerate(ratios)
        )
        inverse = 1.0 / total
        shares = [ratio * inverse for ratio in ratios]
        for section in range(3):
            weights[section, head] = jnp.broadcast_to(shares[section], (8, block))
        wide = sum(share * parts[section, head, 0:hd] for section, share in enumerate(shares))
        att_wide[head] = wide
        rounded = wide.astype(BF16).astype(F32)
        upstream = gt[head].astype(F32)
        return (
            sums[0] + jnp.sum(rounded * rounded, axis=0, keepdims=True),
            sums[1] + jnp.sum(rounded * upstream, axis=0, keepdims=True),
        )

    zero_row = jnp.zeros((1, block), F32)
    square_sum, cross_sum = lax.fori_loop(0, group, merge, (zero_row, zero_row))
    stat_send[...] = jnp.concatenate(
        [square_sum, cross_sum, jnp.zeros((6, block), F32)], axis=0
    )

    @pl.loop(1, members)
    def _(step):
        send(stat_send, stat_recv.at[slot], stat_sems.at[0], stat_sems.at[1], member(step))

    stat_recv[slot] = stat_send[...]
    drain(stat_recv.at[pl.ds(0, members - 1)], stat_sems.at[1])
    stats = stat_recv[0]
    for at in range(1, members):
        stats = stats + stat_recv[at]
    features = HEADS * HEAD_DIM
    rscale = lax.rsqrt(stats[0:1] / features + EPSILON)
    factor = rscale * rscale * rscale * (stats[1:2] / features)

    @pl.loop(0, group)
    def _(head):
        wide = att_wide[head]
        rounded = wide.astype(BF16).astype(F32)
        upstream = gt[head].astype(F32)
        lanes = aligned(head * hd, hd, hd)
        grad = (rscale * upstream - rounded * factor).astype(BF16)
        gat[head] = grad
        ga[head] = grad.T
        delta[head] = jnp.broadcast_to(
            jnp.sum(wide * grad.astype(F32), axis=0, keepdims=True), (8, block)
        )
        nrm[:, lanes] = (rounded * rscale).astype(BF16).T

    def hand_out(number, buffer, out):
        send(
            buffer.at[other_rows, :], out.at[:, own_group],
            out_send.at[number], out_recv.at[number], partner,
        )
        keep = pltpu.make_async_copy(
            buffer.at[own_rows, :], out.at[:, own_group], out_local.at[number]
        )
        keep.start()
        return keep

    keeps = [hand_out(0, nrm, normed_out)]
    dqt[...] = jnp.zeros_like(dqt)

    def backward(section, head):
        values = kv[section * block : (section + 1) * block, hd : 2 * hd]
        dprob = dot(values, gat[head])
        share = probs[section, head].astype(F32) * weights[section, head, 0:1]
        dscore = (share * (dprob - delta[head, 0:1])).astype(BF16)
        lanes = aligned(head * hd, hd, hd)
        dqt[head] += dot(kt[section], dscore)
        dkv[section, :, 0:hd] += dot(dscore, qs[:, lanes])
        dkv[section, :, hd : 2 * hd] += dot(share.astype(BF16), ga[head])

    def backward_section(section):
        dkv[section] = jnp.zeros((block, 2 * hd), F32)

        @pl.loop(0, group)
        def _(head):
            backward(section, head)

    for pick in range(2):
        section = 1 + pick
        backward_section(section)
        dkv_send[pick, :, 0:hd] = (dkv[section, :, 0:hd] * SCALE).astype(BF16)
        dkv_send[pick, :, hd : 2 * hd] = dkv[section, :, hd : 2 * hd].astype(BF16)

        @pl.loop(1, blocks)
        def _(step):
            to = peer(step)
            send(
                dkv_send.at[pick, aligned(piece * to, piece, piece), :],
                arrived.at[pick, aligned(piece * mine, piece, piece), :],
                hop_send.at[3 + pick], hop_recv.at[3 + pick], (2 * to + core, y),
            )

        arrived[pick, aligned(piece * mine, piece, piece), :] = dkv_send[
            pick, aligned(piece * mine, piece, piece), :
        ]

    backward_section(0)

    @pl.loop(0, group)
    def _(head):
        lanes = aligned(head * hd, hd, hd)
        gq[:, lanes] = (dqt[head] * SCALE).astype(BF16).T

    keeps.append(hand_out(1, gq, gq_out))

    for pick in range(2):
        drain(arrived.at[pick, pl.ds(0, block - piece), :], hop_recv.at[3 + pick])
    totals[...] = (dot(table[0], arrived[0]) + dot(table[1], arrived[1])).astype(BF16)

    @pl.loop(1, blocks)
    def _(step):
        to = peer(step)
        send(
            totals.at[aligned(piece * to, piece, piece), :],
            home.at[aligned(piece * mine, piece, piece), :],
            hop_send.at[5], hop_recv.at[5], (2 * to + core, y),
        )

    home[aligned(piece * mine, piece, piece), :] = totals[aligned(piece * mine, piece, piece), :]
    drain(home.at[pl.ds(0, block - piece), :], hop_recv.at[5])
    gkv[:, 0:hd] = (dkv[0, :, 0:hd] * SCALE + home[:, 0:hd].astype(F32)).astype(BF16)
    gkv[:, hd : 2 * hd] = (
        dkv[0, :, hd : 2 * hd] + home[:, hd : 2 * hd].astype(F32)
    ).astype(BF16)

    for number, (lanes, out) in enumerate(((k_lanes, gk_out), (v_lanes, gv_out))):
        send(
            gkv.at[other_rows, lanes], out.at[:, own_head],
            out_send.at[2 + number], out_recv.at[2 + number], partner,
        )
        keep = pltpu.make_async_copy(
            gkv.at[own_rows, lanes], out.at[:, own_head], out_local.at[2 + number]
        )
        keep.start()
        keeps.append(keep)

    for keep in keeps:
        keep.wait()
    for number, (src, dst) in enumerate(swaps):
        drain(src, swap_send.at[number])
    drain(held.at[pl.ds(0, blocks - 1)], hop_send.at[0])
    for pick in range(2):
        drain(picked.at[pick, pl.ds(0, blocks - 1)], hop_send.at[1 + pick])
        drain(dkv_send.at[pick, pl.ds(0, block - piece), :], hop_send.at[3 + pick])
    drain(totals.at[pl.ds(0, block - piece), :], hop_send.at[5])
    drain(stat_recv.at[pl.ds(0, members - 1)], stat_sems.at[0])
    for number, (buffer, out) in enumerate(((nrm, normed_out), (gq, gq_out))):
        drain(buffer.at[other_rows, :], out_send.at[number])
        drain(out.at[:, other_group], out_recv.at[number])
    for number, (lanes, out) in enumerate(((k_lanes, gk_out), (v_lanes, gv_out))):
        drain(gkv.at[other_rows, lanes], out_send.at[2 + number])
        drain(out.at[:, other_head], out_recv.at[2 + number])


def shards(query_rows, key_rows, value_rows, grad_out, chosen):
    blocks = chosen.shape[0]
    rows, kv_width = key_rows.shape
    group = query_rows.shape[1] // kv_width
    kvh = lax.axis_size("kvh")
    hd = HEAD_DIM
    block = 2 * rows
    piece = block // blocks
    width = group * hd
    anywhere = pl.BlockSpec(memory_space=pl.ANY)
    scratch = [
        pltpu.VMEM((block, width), BF16),
        pltpu.VMEM((block, width), BF16),
        pltpu.VMEM((3 * block, 2 * hd), BF16),
        pltpu.VMEM((3, hd + 16, block), BF16),
        pltpu.VMEM((3, hd, block), BF16),
        pltpu.VMEM((group, hd, block), BF16),
        pltpu.VMEM((group, hd, block), BF16),
        pltpu.VMEM((blocks, piece, 2 * hd), BF16),
        pltpu.VMEM((2, blocks, piece, 2 * hd), BF16),
        pltpu.VMEM((3, group, block, block), BF16),
        pltpu.VMEM((3, group, 8, block), F32),
        pltpu.VMEM((3, group, hd + 16, block), F32),
        pltpu.VMEM((3, group, 8, block), F32),
        pltpu.VMEM((group, hd, block), F32),
        pltpu.VMEM((8, block), F32),
        pltpu.VMEM((2 * kvh, 8, block), F32),
        pltpu.VMEM((group, hd, block), BF16),
        pltpu.VMEM((group, block, hd), BF16),
        pltpu.VMEM((group, 8, block), F32),
        pltpu.VMEM((group, hd, block), F32),
        pltpu.VMEM((3, block, 2 * hd), F32),
        pltpu.VMEM((2, block, 2 * hd), BF16),
        pltpu.VMEM((2, block, 2 * hd), BF16),
        pltpu.VMEM((2, block, block), BF16),
        pltpu.VMEM((block, 2 * hd), BF16),
        pltpu.VMEM((block, 2 * hd), BF16),
        pltpu.VMEM((block, width), BF16),
        pltpu.VMEM((block, width), BF16),
        pltpu.VMEM((block, 2 * hd), BF16),
        pltpu.SemaphoreType.DMA((4,)),
        pltpu.SemaphoreType.DMA((4,)),
        pltpu.SemaphoreType.DMA((4,)),
        pltpu.SemaphoreType.DMA((6,)),
        pltpu.SemaphoreType.DMA((6,)),
        pltpu.SemaphoreType.DMA((2,)),
        pltpu.SemaphoreType.DMA((4,)),
        pltpu.SemaphoreType.DMA((4,)),
        pltpu.SemaphoreType.DMA((4,)),
    ]
    return pl.pallas_call(
        functools.partial(kernel, blocks, rows, group, kvh),
        out_shape=(
            jax.ShapeDtypeStruct(query_rows.shape, BF16),
            jax.ShapeDtypeStruct(query_rows.shape, BF16),
            jax.ShapeDtypeStruct(key_rows.shape, BF16),
            jax.ShapeDtypeStruct(key_rows.shape, BF16),
        ),
        in_specs=[pl.BlockSpec(memory_space=pltpu.SMEM)] + [anywhere] * 4,
        out_specs=(anywhere,) * 4,
        scratch_shapes=scratch,
        compiler_params=pltpu.CompilerParams(
            collective_id=0, has_side_effects=True, vmem_limit_bytes=60 * 2**20
        ),
        name="moba",
    )(chosen, query_rows, key_rows, value_rows, grad_out)


def solution(mesh):
    return jax.shard_map(
        shards,
        mesh=mesh,
        in_specs=(P("ctx", "kvh"), P("ctx", "kvh"), P("ctx", "kvh"), P("ctx", "kvh"), P()),
        out_specs=(P("ctx", "kvh"), P("ctx", "kvh"), P("ctx", "kvh"), P("ctx", "kvh")),
        check_vma=False,
    )
```

```python
import functools
import math

import jax
import jax.numpy as jnp
from jax import lax
from jax.experimental import pallas as pl
from jax.experimental.pallas import tpu as pltpu
from jax.sharding import PartitionSpec as P

HEADS = 32
HEAD_DIM = 128
EPSILON = 1e-06
SCALE = 1.0 / math.sqrt(HEAD_DIM)
SCALE2 = SCALE * math.log2(math.e)
MESH = pl.DeviceIdType.MESH
F32 = jnp.float32
BF16 = jnp.bfloat16
NEG = -jnp.inf


def dot(left, right):
    return jnp.dot(left, right, preferred_element_type=F32)


def aligned(start, size, step):
    return pl.ds(pl.multiple_of(start, step), size)


def kernel(
    blocks, rows, group, kvh,
    chosen, q_in, k_in, v_in, g_in,
    normed_out, gq_out, part_k, part_v, home_k, home_v,
    qs, gos, ks, vs, vtx, kt, qt, gt, held_k, held_v, picked_k, picked_v, probs, maxes, parts,
    weights, att_wide, stat_send, stat_recv, gat, ga, delta, dqt, dk, dv, dk_send, dv_send,
    arrived_k, arrived_v, table, totals_k, totals_v, nrm, gq,
    local_sem, swap_send, swap_recv, hop_send, hop_recv, stat_sems, out_local, out_send, out_recv,
):
    hd = HEAD_DIM
    block = 2 * rows
    piece = block // blocks
    width = group * hd
    ctx = lax.axis_index("ctx")
    y = lax.axis_index("kvh")
    mine = ctx // 2
    core = lax.rem(ctx, 2)
    other = 1 - core
    partner = (2 * mine + other, y)
    far = 2 * (kvh - 1)
    half_blocks = blocks // 2
    upper = mine // half_blocks

    def peer(step):
        return lax.rem(mine + step, blocks)

    def far_member(step):
        return (2 * mine + lax.rem(step, 2), lax.rem(y + 1 + step // 2, kvh))

    def drain(ref, sem):
        pltpu.make_async_copy(ref, ref, sem).wait()

    def send(src, dst, send_sem, recv_sem, device):
        pltpu.make_async_remote_copy(
            src_ref=src, dst_ref=dst, send_sem=send_sem, recv_sem=recv_sem,
            device_id=device, device_id_type=MESH,
        ).start()

    def signal(device):
        pl.semaphore_signal(barrier, inc=1, device_id=device, device_id_type=MESH)

    own_rows = aligned(core * rows, rows, rows)
    other_rows = aligned(other * rows, rows, rows)
    own_head = aligned(core * hd, hd, hd)
    other_head = aligned(other * hd, hd, hd)
    own_group = aligned(core * width, width, width)
    other_group = aligned(other * width, width, width)
    my_piece = aligned(piece * mine, piece, piece)

    fetches = [
        pltpu.make_async_copy(k_in.at[:, own_head], ks.at[0, own_rows, :], local_sem.at[0]),
        pltpu.make_async_copy(v_in.at[:, own_head], vs.at[0, own_rows, :], local_sem.at[1]),
        pltpu.make_async_copy(q_in.at[:, own_group], qs.at[own_rows, :], local_sem.at[2]),
        pltpu.make_async_copy(g_in.at[:, own_group], gos.at[own_rows, :], local_sem.at[3]),
    ]
    for fetch in fetches:
        fetch.start()

    barrier = pltpu.get_barrier_semaphore()

    @pl.loop(1, 2 * blocks)
    def _(step):
        signal((lax.rem(ctx + step, 2 * blocks), y))

    @pl.loop(0, far)
    def _(step):
        signal(far_member(step))

    pl.semaphore_wait(barrier, 2 * blocks - 1 + far)

    swaps = [
        (k_in.at[:, other_head], ks.at[0, own_rows, :]),
        (v_in.at[:, other_head], vs.at[0, own_rows, :]),
        (q_in.at[:, other_group], qs.at[own_rows, :]),
        (g_in.at[:, other_group], gos.at[own_rows, :]),
    ]
    for number, (src, dst) in enumerate(swaps):
        send(src, dst, swap_send.at[number], swap_recv.at[number], partner)

    def scatter(number, source, held):
        def scatter_half(half):
            @pl.loop(0, half_blocks)
            def _(step):
                to = half * half_blocks + lax.rem(step + mine, half_blocks)

                @pl.when(to != mine)
                def _():
                    send(
                        source.at[0, aligned(piece * to, piece, piece), :], held.at[mine],
                        hop_send.at[number], hop_recv.at[number], (2 * to + core, y),
                    )

        fetches[number].wait()
        scatter_half(core)
        drain(source.at[0, other_rows, :], swap_recv.at[number])
        scatter_half(other)
        held[mine] = source[0, my_piece, :]

    scatter(0, ks, held_k)
    scatter(1, vs, held_v)

    for number, target in ((2, qs), (3, gos)):
        fetches[number].wait()
        drain(target.at[other_rows, :], swap_recv.at[number])

    def turn_keys(section):
        kt[section] = ks[section].T

    def turn_values(section):
        vtx[section, 0:hd, :] = vs[section].T
        vtx[section, hd : hd + 16, :] = jnp.ones((16, block), BF16)

    def score(section, head):
        scores = dot(ks[section], qt[head])
        if section == 0:
            key_at = lax.broadcasted_iota(jnp.int32, (block, block), 0)
            row_at = lax.broadcasted_iota(jnp.int32, (block, block), 1)
            key_order = 2 * lax.rem(key_at, rows) + key_at // rows
            row_order = 2 * lax.rem(row_at, rows) + row_at // rows
            scores = jnp.where(key_order <= row_order, scores, NEG)
        top = jnp.max(scores, axis=0, keepdims=True)
        terms = jnp.exp2((scores - top) * SCALE2).astype(BF16)
        probs[section, head] = terms
        maxes[section, head] = jnp.broadcast_to(top, (8, block))
        return terms

    def deliver(number, held, picked, target):
        drain(held.at[pl.ds(0, blocks - 1)], hop_recv.at[number])

        @pl.loop(1, blocks)
        def _(step):
            to = peer(step)
            for pick in range(2):
                picked[to, pick] = held[chosen[pick, to]]
            send(
                picked.at[to], target.at[pl.ds(1, 2), my_piece, :],
                hop_send.at[2 + number], hop_recv.at[2 + number], (2 * to + core, y),
            )

        for pick in range(2):
            target[1 + pick, my_piece, :] = held[chosen[pick, mine]]

    turn_keys(0)

    @pl.loop(0, group)
    def _(head):
        qt[head] = qs[:, aligned(head * hd, hd, hd)].T

    deliver(0, held_k, picked_k, ks)
    turn_values(0)

    @pl.loop(0, group)
    def _(head):
        gt[head] = gos[:, aligned(head * hd, hd, hd)].T

    deliver(1, held_v, picked_v, vs)

    @pl.loop(0, group)
    def _(head):
        parts[0, head] = dot(vtx[0], score(0, head))

    for pick in range(2):
        lane_owner = lax.broadcasted_iota(jnp.int32, (8, block), 1) // piece

        def fill(reader, owners):
            choice = chosen[pick, reader]
            choice = jnp.where(choice < reader, choice, -1)
            return jnp.where(lane_owner == reader, choice, owners)

        owners = lax.fori_loop(0, blocks, fill, jnp.full((8, block), -1, jnp.int32))
        row_at = lax.broadcasted_iota(jnp.int32, (block, block), 0)
        lane_at = lax.broadcasted_iota(jnp.int32, (block, block), 1)
        wanted = owners[0:1] * piece + lax.rem(lane_at, piece)
        table[pick] = (row_at == wanted).astype(F32).astype(BF16)

    drain(ks.at[pl.ds(1, 2), pl.ds(0, block - piece), :], hop_recv.at[2])
    for pick in range(2):
        @pl.loop(0, group)
        def _(head):
            score(1 + pick, head)

        turn_keys(1 + pick)

    drain(vs.at[pl.ds(1, 2), pl.ds(0, block - piece), :], hop_recv.at[3])
    for pick in range(2):
        turn_values(1 + pick)

        @pl.loop(0, group)
        def _(head):
            parts[1 + pick, head] = dot(vtx[1 + pick], probs[1 + pick, head])

    valid = [chosen[pick, mine] < mine for pick in range(2)]

    def merge(head, sums):
        top_own = maxes[0, head, 0:1]
        tops = [top_own] + [
            jnp.where(valid[pick], maxes[1 + pick, head, 0:1], NEG) for pick in range(2)
        ]
        top = jnp.maximum(jnp.maximum(tops[0], tops[1]), tops[2])
        ratios = [jnp.exp2((value - top) * SCALE2) for value in tops]
        total = sum(
            ratio * parts[section, head, hd : hd + 1] for section, ratio in enumerate(ratios)
        )
        inverse = 1.0 / total
        shares = [ratio * inverse for ratio in ratios]
        for section in range(3):
            weights[section, head] = jnp.broadcast_to(shares[section], (8, block))
        wide = sum(share * parts[section, head, 0:hd] for section, share in enumerate(shares))
        att_wide[head] = wide
        rounded = wide.astype(BF16).astype(F32)
        upstream = gt[head].astype(F32)
        return (
            sums[0] + jnp.sum(rounded * rounded, axis=0, keepdims=True),
            sums[1] + jnp.sum(rounded * upstream, axis=0, keepdims=True),
        )

    zero_row = jnp.zeros((1, block), F32)
    square_sum, cross_sum = lax.fori_loop(0, group, merge, (zero_row, zero_row))
    stat_send[...] = jnp.concatenate(
        [square_sum, cross_sum, jnp.zeros((6, block), F32)], axis=0
    )
    slot = 2 * y + core
    send(stat_send, stat_recv.at[slot], stat_sems.at[0], stat_sems.at[1], partner)

    @pl.loop(0, far)
    def _(step):
        send(stat_send, stat_recv.at[slot], stat_sems.at[0], stat_sems.at[1], far_member(step))

    stat_recv[slot] = stat_send[...]
    drain(stat_recv.at[pl.ds(0, far + 1)], stat_sems.at[1])
    stats = stat_recv[0]
    for at in range(1, far + 2):
        stats = stats + stat_recv[at]
    features = HEADS * HEAD_DIM
    rscale = lax.rsqrt(stats[0:1] / features + EPSILON)
    factor = rscale * rscale * rscale * (stats[1:2] / features)

    @pl.loop(0, group)
    def _(head):
        wide = att_wide[head]
        rounded = wide.astype(BF16).astype(F32)
        upstream = gt[head].astype(F32)
        grad = (rscale * upstream - rounded * factor).astype(BF16)
        gat[head] = grad
        ga[head] = grad.T
        delta[head] = jnp.broadcast_to(
            jnp.sum(wide * grad.astype(F32), axis=0, keepdims=True), (8, block)
        )

    def value_grad(section):
        dv[...] = jnp.zeros_like(dv)

        @pl.loop(0, group)
        def _(head):
            share = (probs[section, head].astype(F32) * weights[section, head, 0:1]).astype(BF16)
            probs[section, head] = share
            dv[...] += dot(share, ga[head])

    def key_grad(section, first):
        dk[...] = jnp.zeros_like(dk)

        @pl.loop(0, group)
        def _(head):
            dprob = dot(vs[section], gat[head])
            share = probs[section, head].astype(F32)
            dscore = (share * (dprob - delta[head, 0:1])).astype(BF16)
            term = dot(kt[section], dscore)
            if first:
                dqt[head] = term
            else:
                dqt[head] += term
            dk[...] += dot(dscore, qs[:, aligned(head * hd, hd, hd)])

    def give_back(number, pick, source, arrived):
        @pl.loop(1, blocks)
        def _(step):
            to = peer(step)
            send(
                source.at[pick, aligned(piece * to, piece, piece), :],
                arrived.at[pick, my_piece, :],
                hop_send.at[number], hop_recv.at[number], (2 * to + core, y),
            )

        arrived[pick, my_piece, :] = source[pick, my_piece, :]

    for pick in range(2):
        value_grad(1 + pick)
        dv_send[pick] = dv[...].astype(BF16)
        give_back(4 + pick, pick, dv_send, arrived_v)
    for pick in range(2):
        key_grad(1 + pick, pick == 0)
        dk_send[pick] = (dk[...] * SCALE).astype(BF16)
        give_back(6 + pick, pick, dk_send, arrived_k)

    def hand_out(number, buffer, out, lanes):
        send(
            buffer.at[other_rows, :], out.at[:, lanes],
            out_send.at[number], out_recv.at[number], partner,
        )
        keep = pltpu.make_async_copy(
            buffer.at[own_rows, :], out.at[:, lanes], out_local.at[number]
        )
        keep.start()
        return keep

    def settle(number, first_arrival, arrived, totals, home):
        for pick in range(2):
            drain(arrived.at[pick, pl.ds(0, block - piece), :], hop_recv.at[first_arrival + pick])
        totals[...] = (dot(table[0], arrived[0]) + dot(table[1], arrived[1])).astype(BF16)
        target = home.at[aligned(piece * lax.rem(mine, half_blocks), piece, piece), own_head]

        @pl.loop(1, blocks)
        def _(step):
            to = peer(step)
            send(
                totals.at[aligned(piece * to, piece, piece), :], target,
                hop_send.at[number], hop_recv.at[number], (2 * to + upper, y),
            )

        @pl.when(upper != core)
        def _():
            send(
                totals.at[my_piece, :], target,
                hop_send.at[number], hop_recv.at[number], partner,
            )

        @pl.when(upper == core)
        def _():
            pltpu.make_async_copy(totals.at[my_piece, :], target, hop_recv.at[number]).start()

    value_grad(0)
    keeps = [hand_out(0, dv, part_v, own_head)]
    key_grad(0, False)
    dk[...] = dk[...] * SCALE
    keeps.append(hand_out(1, dk, part_k, own_head))
    settle(8, 4, arrived_v, totals_v, home_v)

    @pl.loop(0, group)
    def _(head):
        lanes = aligned(head * hd, hd, hd)
        gq[:, lanes] = (dqt[head] * SCALE).astype(BF16).T

    keeps.append(hand_out(2, gq, gq_out, own_group))

    @pl.loop(0, group)
    def _(head):
        lanes = aligned(head * hd, hd, hd)
        nrm[:, lanes] = (att_wide[head].astype(BF16).astype(F32) * rscale).astype(BF16).T

    keeps.append(hand_out(3, nrm, normed_out, own_group))
    settle(9, 6, arrived_k, totals_k, home_k)

    for number, (src, _) in enumerate(swaps):
        drain(src, swap_send.at[number])
    drain(held_k.at[pl.ds(0, blocks - 1)], hop_send.at[0])
    drain(held_v.at[pl.ds(0, blocks - 1)], hop_send.at[1])
    drain(picked_k.at[pl.ds(0, blocks - 1)], hop_send.at[2])
    drain(picked_v.at[pl.ds(0, blocks - 1)], hop_send.at[3])
    for number in range(4):
        drain(dv_send.at[0, pl.ds(0, block - piece), :], hop_send.at[4 + number])
    drain(stat_recv.at[pl.ds(0, far + 1)], stat_sems.at[0])
    for keep in keeps:
        keep.wait()
    for number, (buffer, out, lanes) in enumerate((
        (dv, part_v, other_head), (dk, part_k, other_head),
        (gq, gq_out, other_group), (nrm, normed_out, other_group),
    )):
        drain(buffer.at[other_rows, :], out_send.at[number])
        drain(out.at[:, lanes], out_recv.at[number])
    for number in (8, 9):
        drain(totals_k.at[pl.ds(0, block - piece), :], hop_send.at[number])

        @pl.when(upper != core)
        def _():
            drain(totals_k.at[my_piece, :], hop_send.at[number])

    drain(home_v, hop_recv.at[8])
    drain(home_k, hop_recv.at[9])


def finish(
    normed_in, gq_in, part_k, part_v, home_k, home_v,
    normed_out, gq_out, gk_out, gv_out,
    wides, parts, homes, grads, in_sems, part_sems, home_sems, out_sems, grad_sems,
):
    chunks = wides.shape[1]
    rows = wides.shape[2]
    loads = []
    stores = []
    for number, (src, dst) in enumerate(((normed_in, normed_out), (gq_in, gq_out))):
        for at in range(chunks):
            span = pl.ds(at * rows, rows)
            held = wides.at[number, at]
            loads.append(pltpu.make_async_copy(src.at[span, :], held, in_sems.at[number, at]))
            stores.append(pltpu.make_async_copy(held, dst.at[span, :], out_sems.at[number, at]))
    terms = []
    for number, (part, home) in enumerate(((part_k, home_k), (part_v, home_v))):
        terms.append((
            pltpu.make_async_copy(part, parts.at[number], part_sems.at[number]),
            pltpu.make_async_copy(home, homes.at[number], home_sems.at[number]),
        ))
    for load in loads:
        load.start()
    for part_load, home_load in terms:
        part_load.start()
        home_load.start()
    for load, store in zip(loads, stores):
        load.wait()
        store.start()
    for number, out in enumerate((gk_out, gv_out)):
        terms[number][0].wait()
        terms[number][1].wait()
        grads[number] = (parts[number] + homes[number].astype(F32)).astype(BF16)
        store = pltpu.make_async_copy(grads.at[number], out, grad_sems.at[number])
        store.start()
        stores.append(store)
    for store in stores:
        store.wait()


def shards(query_rows, key_rows, value_rows, grad_out, chosen):
    blocks = chosen.shape[0]
    rows, kv_width = key_rows.shape
    group = query_rows.shape[1] // kv_width
    kvh = lax.axis_size("kvh")
    hd = HEAD_DIM
    block = 2 * rows
    piece = block // blocks
    width = group * hd
    anywhere = pl.BlockSpec(memory_space=pl.ANY)
    scratch = [
        pltpu.VMEM((block, width), BF16),
        pltpu.VMEM((block, width), BF16),
        pltpu.VMEM((3, block, hd), BF16),
        pltpu.VMEM((3, block, hd), BF16),
        pltpu.VMEM((3, hd + 16, block), BF16),
        pltpu.VMEM((3, hd, block), BF16),
        pltpu.VMEM((group, hd, block), BF16),
        pltpu.VMEM((group, hd, block), BF16),
        pltpu.VMEM((blocks, piece, hd), BF16),
        pltpu.VMEM((blocks, piece, hd), BF16),
        pltpu.VMEM((blocks, 2, piece, hd), BF16),
        pltpu.VMEM((blocks, 2, piece, hd), BF16),
        pltpu.VMEM((3, group, block, block), BF16),
        pltpu.VMEM((3, group, 8, block), F32),
        pltpu.VMEM((3, group, hd + 16, block), F32),
        pltpu.VMEM((3, group, 8, block), F32),
        pltpu.VMEM((group, hd, block), F32),
        pltpu.VMEM((8, block), F32),
        pltpu.VMEM((2 * kvh, 8, block), F32),
        pltpu.VMEM((group, hd, block), BF16),
        pltpu.VMEM((group, block, hd), BF16),
        pltpu.VMEM((group, 8, block), F32),
        pltpu.VMEM((group, hd, block), F32),
        pltpu.VMEM((block, hd), F32),
        pltpu.VMEM((block, hd), F32),
        pltpu.VMEM((2, block, hd), BF16),
        pltpu.VMEM((2, block, hd), BF16),
        pltpu.VMEM((2, block, hd), BF16),
        pltpu.VMEM((2, block, hd), BF16),
        pltpu.VMEM((2, block, block), BF16),
        pltpu.VMEM((block, hd), BF16),
        pltpu.VMEM((block, hd), BF16),
        pltpu.VMEM((block, width), BF16),
        pltpu.VMEM((block, width), BF16),
        pltpu.SemaphoreType.DMA((4,)),
        pltpu.SemaphoreType.DMA((4,)),
        pltpu.SemaphoreType.DMA((4,)),
        pltpu.SemaphoreType.DMA((10,)),
        pltpu.SemaphoreType.DMA((10,)),
        pltpu.SemaphoreType.DMA((2,)),
        pltpu.SemaphoreType.DMA((4,)),
        pltpu.SemaphoreType.DMA((4,)),
        pltpu.SemaphoreType.DMA((4,)),
    ]
    wide = jax.ShapeDtypeStruct(query_rows.shape, BF16)
    part = jax.ShapeDtypeStruct(key_rows.shape, F32)
    thin = jax.ShapeDtypeStruct(key_rows.shape, BF16)
    results = pl.pallas_call(
        functools.partial(kernel, blocks, rows, group, kvh),
        out_shape=(wide, wide, part, part, thin, thin),
        in_specs=[pl.BlockSpec(memory_space=pltpu.SMEM)] + [anywhere] * 4,
        out_specs=(anywhere,) * 6,
        scratch_shapes=scratch,
        compiler_params=pltpu.CompilerParams(
            collective_id=0, has_side_effects=True, vmem_limit_bytes=60 * 2**20
        ),
        name="moba",
    )(chosen.T, query_rows, key_rows, value_rows, grad_out)
    return pl.pallas_call(
        finish,
        out_shape=(wide, wide, thin, thin),
        in_specs=[anywhere] * 6,
        out_specs=(anywhere,) * 4,
        scratch_shapes=[
            pltpu.VMEM((2, 4, rows // 4, query_rows.shape[1]), BF16),
            pltpu.VMEM((2, *key_rows.shape), F32),
            pltpu.VMEM((2, *key_rows.shape), BF16),
            pltpu.VMEM((2, *key_rows.shape), BF16),
            pltpu.SemaphoreType.DMA((2, 4)),
            pltpu.SemaphoreType.DMA((2,)),
            pltpu.SemaphoreType.DMA((2,)),
            pltpu.SemaphoreType.DMA((2, 4)),
            pltpu.SemaphoreType.DMA((2,)),
        ],
        name="finish",
    )(*results)


def solution(mesh):
    return jax.shard_map(
        shards,
        mesh=mesh,
        in_specs=(P("ctx", "kvh"), P("ctx", "kvh"), P("ctx", "kvh"), P("ctx", "kvh"), P()),
        out_specs=(P("ctx", "kvh"), P("ctx", "kvh"), P("ctx", "kvh"), P("ctx", "kvh")),
        check_vma=False,
    )
```

```python
import functools
import math

import jax
import jax.numpy as jnp
from jax import lax
from jax.experimental import pallas as pl
from jax.experimental.pallas import tpu as pltpu
from jax.sharding import PartitionSpec as P

HEADS = 32
HEAD_DIM = 128
EPSILON = 1e-06
SCALE = 1.0 / math.sqrt(HEAD_DIM)
SCALE2 = SCALE * math.log2(math.e)
MESH = pl.DeviceIdType.MESH
F32 = jnp.float32
BF16 = jnp.bfloat16
NEG = -jnp.inf


def dot(left, right):
    return jnp.dot(left, right, preferred_element_type=F32)


def aligned(start, size, step):
    return pl.ds(pl.multiple_of(start, step), size)


def kernel(
    blocks, rows, group, kvh,
    chosen, q_in, k_in, v_in, g_in,
    normed_out, gq_out, part_k, part_v, home_k, home_v,
    qs, gos, ks, vs, vtx, kt, qh, qt, gt, held_k, held_v, picked_k, picked_v, probs, maxes, parts,
    weights, att_wide, stat_send, stat_recv, gat, ga, delta, dscores, dk, dv, dk_send, dv_send,
    arrived_k, arrived_v, table, totals_k, totals_v, nrm, gq,
    local_sem, swap_send, swap_recv, hop_send, hop_recv, stat_sems, out_local, out_send, out_recv,
):
    hd = HEAD_DIM
    block = 2 * rows
    piece = block // blocks
    width = group * hd
    ctx = lax.axis_index("ctx")
    y = lax.axis_index("kvh")
    mine = ctx // 2
    core = lax.rem(ctx, 2)
    other = 1 - core
    partner = (2 * mine + other, y)
    far = 2 * (kvh - 1)
    half_blocks = blocks // 2
    upper = mine // half_blocks

    def peer(step):
        return lax.rem(mine + step, blocks)

    def far_member(step):
        return (2 * mine + lax.rem(step, 2), lax.rem(y + 1 + step // 2, kvh))

    def drain(ref, sem):
        pltpu.make_async_copy(ref, ref, sem).wait()

    def send(src, dst, send_sem, recv_sem, device):
        pltpu.make_async_remote_copy(
            src_ref=src, dst_ref=dst, send_sem=send_sem, recv_sem=recv_sem,
            device_id=device, device_id_type=MESH,
        ).start()

    def signal(device):
        pl.semaphore_signal(barrier, inc=1, device_id=device, device_id_type=MESH)

    own_rows = aligned(core * rows, rows, rows)
    other_rows = aligned(other * rows, rows, rows)
    own_head = aligned(core * hd, hd, hd)
    other_head = aligned(other * hd, hd, hd)
    own_group = aligned(core * width, width, width)
    other_group = aligned(other * width, width, width)
    my_piece = aligned(piece * mine, piece, piece)

    fetches = [
        pltpu.make_async_copy(k_in.at[:, own_head], ks.at[0, own_rows, :], local_sem.at[0]),
        pltpu.make_async_copy(v_in.at[:, own_head], vs.at[0, own_rows, :], local_sem.at[1]),
        pltpu.make_async_copy(q_in.at[:, own_group], qs.at[own_rows, :], local_sem.at[2]),
        pltpu.make_async_copy(g_in.at[:, own_group], gos.at[own_rows, :], local_sem.at[3]),
    ]
    for fetch in fetches:
        fetch.start()

    barrier = pltpu.get_barrier_semaphore()

    @pl.loop(1, 2 * blocks)
    def _(step):
        signal((lax.rem(ctx + step, 2 * blocks), y))

    @pl.loop(0, far)
    def _(step):
        signal(far_member(step))

    pl.semaphore_wait(barrier, 2 * blocks - 1 + far)

    swaps = [
        (k_in.at[:, other_head], ks.at[0, own_rows, :]),
        (v_in.at[:, other_head], vs.at[0, own_rows, :]),
        (q_in.at[:, other_group], qs.at[own_rows, :]),
        (g_in.at[:, other_group], gos.at[own_rows, :]),
    ]

    def swap(number):
        src, dst = swaps[number]
        send(src, dst, swap_send.at[number], swap_recv.at[number], partner)

    swap(0)
    swap(1)

    def scatter(number, source, held):
        def scatter_half(half):
            @pl.loop(0, half_blocks)
            def _(step):
                to = half * half_blocks + lax.rem(step + mine, half_blocks)

                @pl.when(to != mine)
                def _():
                    send(
                        source.at[0, aligned(piece * to, piece, piece), :], held.at[mine],
                        hop_send.at[number], hop_recv.at[number], (2 * to + core, y),
                    )

        fetches[number].wait()
        scatter_half(core)
        drain(source.at[0, other_rows, :], swap_recv.at[number])
        scatter_half(other)
        held[mine] = source[0, my_piece, :]

    scatter(0, ks, held_k)
    drain(held_k.at[pl.ds(0, blocks - 1)], hop_send.at[0])
    scatter(1, vs, held_v)
    swap(2)
    swap(3)

    for number, target in ((2, qs), (3, gos)):
        fetches[number].wait()
        drain(target.at[other_rows, :], swap_recv.at[number])

    def turn_keys(section):
        kt[:, section * block : (section + 1) * block] = ks[section].T

    def turn_values(section):
        vtx[section, 0:hd, :] = vs[section].T
        vtx[section, hd : hd + 16, :] = jnp.ones((16, block), BF16)

    def head_lanes(head):
        return aligned(head * block, block, block)

    def score(section, head):
        scores = dot(ks[section], qt[head])
        if section == 0:
            key_at = lax.broadcasted_iota(jnp.int32, (block, block), 0)
            row_at = lax.broadcasted_iota(jnp.int32, (block, block), 1)
            key_order = 2 * lax.rem(key_at, rows) + key_at // rows
            row_order = 2 * lax.rem(row_at, rows) + row_at // rows
            scores = jnp.where(key_order <= row_order, scores, NEG)
        top = jnp.max(scores, axis=0, keepdims=True)
        terms = jnp.exp2((scores - top) * SCALE2).astype(BF16)
        probs[section, :, head_lanes(head)] = terms
        maxes[section, head] = jnp.broadcast_to(top, (8, block))
        return terms

    def deliver_keys():
        drain(held_k.at[pl.ds(0, blocks - 1)], hop_recv.at[0])

        @pl.loop(1, blocks)
        def _(step):
            to = peer(step)
            for pick in range(2):
                picked_k[to, pick] = held_k[chosen[pick, to]]
            send(
                picked_k.at[to], ks.at[pl.ds(1, 2), my_piece, :],
                hop_send.at[2], hop_recv.at[2], (2 * to + core, y),
            )

        for pick in range(2):
            ks[1 + pick, my_piece, :] = held_k[chosen[pick, mine]]

    def deliver_values(pick):
        @pl.loop(1, blocks)
        def _(step):
            to = peer(step)
            picked_v[pick, to] = held_v[chosen[pick, to]]
            send(
                picked_v.at[pick, to], vs.at[1 + pick, my_piece, :],
                hop_send.at[3 + pick], hop_recv.at[3 + pick], (2 * to + core, y),
            )

        vs[1 + pick, my_piece, :] = held_v[chosen[pick, mine]]

    turn_keys(0)

    @pl.loop(0, group)
    def _(head):
        queries = qs[:, aligned(head * hd, hd, hd)]
        qh[aligned(head * block, block, block), :] = queries
        qt[head] = queries.T

    drain(held_v.at[pl.ds(0, blocks - 1)], hop_send.at[1])
    deliver_keys()
    turn_values(0)

    @pl.loop(0, group)
    def _(head):
        gt[head] = gos[:, aligned(head * hd, hd, hd)].T

    @pl.loop(0, group)
    def _(head):
        parts[0, head] = dot(vtx[0], score(0, head))

    drain(held_v.at[pl.ds(0, blocks - 1)], hop_recv.at[1])
    drain(picked_k.at[pl.ds(0, blocks - 1)], hop_send.at[2])
    deliver_values(0)

    for pick in range(2):
        lane_owner = lax.broadcasted_iota(jnp.int32, (8, block), 1) // piece

        def fill(reader, owners):
            choice = chosen[pick, reader]
            choice = jnp.where(choice < reader, choice, -1)
            return jnp.where(lane_owner == reader, choice, owners)

        owners = lax.fori_loop(0, blocks, fill, jnp.full((8, block), -1, jnp.int32))
        row_at = lax.broadcasted_iota(jnp.int32, (block, block), 0)
        lane_at = lax.broadcasted_iota(jnp.int32, (block, block), 1)
        wanted = owners[0:1] * piece + lax.rem(lane_at, piece)
        table[pick] = (row_at == wanted).astype(F32).astype(BF16)

    drain(picked_v.at[0, pl.ds(0, blocks - 1)], hop_send.at[3])
    deliver_values(1)
    drain(ks.at[pl.ds(1, 2), pl.ds(0, block - piece), :], hop_recv.at[2])
    for pick in range(2):
        @pl.loop(0, group)
        def _(head):
            score(1 + pick, head)

        turn_keys(1 + pick)

    for pick in range(2):
        drain(vs.at[1 + pick, pl.ds(0, block - piece), :], hop_recv.at[3 + pick])
        turn_values(1 + pick)

        @pl.loop(0, group)
        def _(head):
            parts[1 + pick, head] = dot(vtx[1 + pick], probs[1 + pick, :, head_lanes(head)])

    valid = [chosen[pick, mine] < mine for pick in range(2)]

    def merge(head, sums):
        top_own = maxes[0, head, 0:1]
        tops = [top_own] + [
            jnp.where(valid[pick], maxes[1 + pick, head, 0:1], NEG) for pick in range(2)
        ]
        top = jnp.maximum(jnp.maximum(tops[0], tops[1]), tops[2])
        ratios = [jnp.exp2((value - top) * SCALE2) for value in tops]
        total = sum(
            ratio * parts[section, head, hd : hd + 1] for section, ratio in enumerate(ratios)
        )
        inverse = 1.0 / total
        shares = [ratio * inverse for ratio in ratios]
        for section in range(3):
            weights[section, head] = jnp.broadcast_to(shares[section], (8, block))
        wide = sum(share * parts[section, head, 0:hd] for section, share in enumerate(shares))
        att_wide[head] = wide
        rounded = wide.astype(BF16).astype(F32)
        upstream = gt[head].astype(F32)
        return (
            sums[0] + jnp.sum(rounded * rounded, axis=0, keepdims=True),
            sums[1] + jnp.sum(rounded * upstream, axis=0, keepdims=True),
        )

    zero_row = jnp.zeros((1, block), F32)
    square_sum, cross_sum = lax.fori_loop(0, group, merge, (zero_row, zero_row))
    folds = block // 128
    stat_send[...] = jnp.concatenate(
        [
            total[:, at * 128 : (at + 1) * 128]
            for total in (square_sum, cross_sum)
            for at in range(folds)
        ],
        axis=0,
    )
    slot = 2 * y + core
    send(stat_send, stat_recv.at[slot], stat_sems.at[0], stat_sems.at[1], partner)

    @pl.loop(0, far)
    def _(step):
        send(stat_send, stat_recv.at[slot], stat_sems.at[0], stat_sems.at[1], far_member(step))

    stat_recv[slot] = stat_send[...]

    @pl.loop(0, group)
    def _(head):
        lanes = head_lanes(head)
        for section in range(3):
            share = probs[section, :, lanes].astype(F32) * weights[section, head, 0:1]
            probs[section, :, lanes] = share.astype(BF16)

    drain(stat_recv.at[pl.ds(0, far + 1)], stat_sems.at[1])
    stats = stat_recv[0]
    for at in range(1, far + 2):
        stats = stats + stat_recv[at]
    features = HEADS * HEAD_DIM
    square_row = jnp.concatenate([stats[at : at + 1] for at in range(folds)], axis=1)
    cross_row = jnp.concatenate([stats[folds + at : folds + at + 1] for at in range(folds)], axis=1)
    rscale = lax.rsqrt(square_row / features + EPSILON)
    factor = rscale * rscale * rscale * (cross_row / features)

    @pl.loop(0, group)
    def _(head):
        wide = att_wide[head]
        rounded = wide.astype(BF16).astype(F32)
        upstream = gt[head].astype(F32)
        grad = (rscale * upstream - rounded * factor).astype(BF16)
        gat[head] = grad
        ga[head_lanes(head), :] = grad.T
        delta[head] = jnp.broadcast_to(
            jnp.sum(wide * grad.astype(F32), axis=0, keepdims=True), (8, block)
        )

    def value_grad(section):
        return dot(probs[section], ga[...])

    def key_grad(section):
        @pl.loop(0, group)
        def _(head):
            lanes = head_lanes(head)
            dprob = dot(vs[section], gat[head])
            share = probs[section, :, lanes].astype(F32)
            dscore = (share * (dprob - delta[head, 0:1])).astype(BF16)
            dscores[section * block : (section + 1) * block, lanes] = dscore

        return dot(dscores[section * block : (section + 1) * block, :], qh[...]) * SCALE

    def give_back(number, pick, source, arrived):
        @pl.loop(1, blocks)
        def _(step):
            to = peer(step)
            send(
                source.at[pick, aligned(piece * to, piece, piece), :],
                arrived.at[pick, my_piece, :],
                hop_send.at[number], hop_recv.at[number], (2 * to + core, y),
            )

        arrived[pick, my_piece, :] = source[pick, my_piece, :]

    for pick in range(2):
        dv_send[pick] = value_grad(1 + pick).astype(BF16)
        give_back(5 + pick, pick, dv_send, arrived_v)
    for pick in range(2):
        dk_send[pick] = key_grad(1 + pick).astype(BF16)
        give_back(7 + pick, pick, dk_send, arrived_k)

    def hand_out(number, buffer, out, lanes):
        send(
            buffer.at[other_rows, :], out.at[:, lanes],
            out_send.at[number], out_recv.at[number], partner,
        )
        keep = pltpu.make_async_copy(
            buffer.at[own_rows, :], out.at[:, lanes], out_local.at[number]
        )
        keep.start()
        return keep

    def settle(number, arrival, arrived, totals, home):
        for pick in range(2):
            drain(arrived.at[pick, pl.ds(0, block - piece), :], hop_recv.at[arrival + pick])
        totals[...] = (dot(table[0], arrived[0]) + dot(table[1], arrived[1])).astype(BF16)
        target = home.at[aligned(piece * lax.rem(mine, half_blocks), piece, piece), own_head]

        @pl.loop(1, blocks)
        def _(step):
            to = peer(step)
            send(
                totals.at[aligned(piece * to, piece, piece), :], target,
                hop_send.at[number], hop_recv.at[number], (2 * to + upper, y),
            )

        @pl.when(upper != core)
        def _():
            send(
                totals.at[my_piece, :], target,
                hop_send.at[number], hop_recv.at[number], partner,
            )

        @pl.when(upper == core)
        def _():
            pltpu.make_async_copy(totals.at[my_piece, :], target, hop_recv.at[number]).start()

    dv[...] = value_grad(0)
    keeps = [hand_out(0, dv, part_v, own_head)]
    dk[...] = key_grad(0)
    keeps.append(hand_out(1, dk, part_k, own_head))
    settle(9, 5, arrived_v, totals_v, home_v)

    @pl.loop(0, group)
    def _(head):
        lanes = aligned(head * hd, hd, hd)
        grad = dot(kt[...], dscores[:, head_lanes(head)]) * SCALE
        gq[:, lanes] = grad.astype(BF16).T

    keeps.append(hand_out(2, gq, gq_out, own_group))

    @pl.loop(0, group)
    def _(head):
        lanes = aligned(head * hd, hd, hd)
        nrm[:, lanes] = (att_wide[head].astype(BF16).astype(F32) * rscale).astype(BF16).T

    keeps.append(hand_out(3, nrm, normed_out, own_group))
    settle(10, 7, arrived_k, totals_k, home_k)

    for number, (src, _) in enumerate(swaps):
        drain(src, swap_send.at[number])
    drain(picked_v.at[1, pl.ds(0, blocks - 1)], hop_send.at[4])
    for number, buffer in ((5, dv_send), (7, dk_send)):
        for pick in range(2):
            drain(buffer.at[pick, pl.ds(0, block - piece), :], hop_send.at[number + pick])
    drain(stat_recv.at[pl.ds(0, far + 1)], stat_sems.at[0])
    for keep in keeps:
        keep.wait()
    for number, (buffer, out, lanes) in enumerate((
        (dv, part_v, other_head), (dk, part_k, other_head),
        (gq, gq_out, other_group), (nrm, normed_out, other_group),
    )):
        drain(buffer.at[other_rows, :], out_send.at[number])
        drain(out.at[:, lanes], out_recv.at[number])
    for number in (9, 10):
        drain(totals_k.at[pl.ds(0, block - piece), :], hop_send.at[number])

        @pl.when(upper != core)
        def _():
            drain(totals_k.at[my_piece, :], hop_send.at[number])

    drain(home_v, hop_recv.at[9])
    drain(home_k, hop_recv.at[10])


def finish(
    normed_in, gq_in, part_k, part_v, home_k, home_v,
    normed_out, gq_out, gk_out, gv_out,
    wides, parts, homes, grads, in_sems, part_sems, home_sems, out_sems, grad_sems,
):
    chunks = wides.shape[1]
    rows = wides.shape[2]
    loads = []
    stores = []
    for number, (src, dst) in enumerate(((normed_in, normed_out), (gq_in, gq_out))):
        for at in range(chunks):
            span = pl.ds(at * rows, rows)
            held = wides.at[number, at]
            loads.append(pltpu.make_async_copy(src.at[span, :], held, in_sems.at[number, at]))
            stores.append(pltpu.make_async_copy(held, dst.at[span, :], out_sems.at[number, at]))
    terms = []
    for number, (part, home) in enumerate(((part_k, home_k), (part_v, home_v))):
        terms.append((
            pltpu.make_async_copy(part, parts.at[number], part_sems.at[number]),
            pltpu.make_async_copy(home, homes.at[number], home_sems.at[number]),
        ))
    for load in loads:
        load.start()
    for part_load, home_load in terms:
        part_load.start()
        home_load.start()
    for load, store in zip(loads, stores):
        load.wait()
        store.start()
    for number, out in enumerate((gk_out, gv_out)):
        terms[number][0].wait()
        terms[number][1].wait()
        grads[number] = (parts[number] + homes[number].astype(F32)).astype(BF16)
        store = pltpu.make_async_copy(grads.at[number], out, grad_sems.at[number])
        store.start()
        stores.append(store)
    for store in stores:
        store.wait()


def shards(query_rows, key_rows, value_rows, grad_out, chosen):
    blocks = chosen.shape[0]
    rows, kv_width = key_rows.shape
    group = query_rows.shape[1] // kv_width
    kvh = lax.axis_size("kvh")
    hd = HEAD_DIM
    block = 2 * rows
    piece = block // blocks
    width = group * hd
    anywhere = pl.BlockSpec(memory_space=pl.ANY)
    scratch = [
        pltpu.VMEM((block, width), BF16),
        pltpu.VMEM((block, width), BF16),
        pltpu.VMEM((3, block, hd), BF16),
        pltpu.VMEM((3, block, hd), BF16),
        pltpu.VMEM((3, hd + 16, block), BF16),
        pltpu.VMEM((hd, 3 * block), BF16),
        pltpu.VMEM((group * block, hd), BF16),
        pltpu.VMEM((group, hd, block), BF16),
        pltpu.VMEM((group, hd, block), BF16),
        pltpu.VMEM((blocks, piece, hd), BF16),
        pltpu.VMEM((blocks, piece, hd), BF16),
        pltpu.VMEM((blocks, 2, piece, hd), BF16),
        pltpu.VMEM((2, blocks, piece, hd), BF16),
        pltpu.VMEM((3, block, group * block), BF16),
        pltpu.VMEM((3, group, 8, block), F32),
        pltpu.VMEM((3, group, hd + 16, block), F32),
        pltpu.VMEM((3, group, 8, block), F32),
        pltpu.VMEM((group, hd, block), F32),
        pltpu.VMEM((2 * block // 128, 128), F32),
        pltpu.VMEM((2 * kvh, 2 * block // 128, 128), F32),
        pltpu.VMEM((group, hd, block), BF16),
        pltpu.VMEM((group * block, hd), BF16),
        pltpu.VMEM((group, 8, block), F32),
        pltpu.VMEM((3 * block, group * block), BF16),
        pltpu.VMEM((block, hd), F32),
        pltpu.VMEM((block, hd), F32),
        pltpu.VMEM((2, block, hd), BF16),
        pltpu.VMEM((2, block, hd), BF16),
        pltpu.VMEM((2, block, hd), BF16),
        pltpu.VMEM((2, block, hd), BF16),
        pltpu.VMEM((2, block, block), BF16),
        pltpu.VMEM((block, hd), BF16),
        pltpu.VMEM((block, hd), BF16),
        pltpu.VMEM((block, width), BF16),
        pltpu.VMEM((block, width), BF16),
        pltpu.SemaphoreType.DMA((4,)),
        pltpu.SemaphoreType.DMA((4,)),
        pltpu.SemaphoreType.DMA((4,)),
        pltpu.SemaphoreType.DMA((11,)),
        pltpu.SemaphoreType.DMA((11,)),
        pltpu.SemaphoreType.DMA((2,)),
        pltpu.SemaphoreType.DMA((4,)),
        pltpu.SemaphoreType.DMA((4,)),
        pltpu.SemaphoreType.DMA((4,)),
    ]
    wide = jax.ShapeDtypeStruct(query_rows.shape, BF16)
    part = jax.ShapeDtypeStruct(key_rows.shape, F32)
    thin = jax.ShapeDtypeStruct(key_rows.shape, BF16)
    results = pl.pallas_call(
        functools.partial(kernel, blocks, rows, group, kvh),
        out_shape=(wide, wide, part, part, thin, thin),
        in_specs=[pl.BlockSpec(memory_space=pltpu.SMEM)] + [anywhere] * 4,
        out_specs=(anywhere,) * 6,
        scratch_shapes=scratch,
        compiler_params=pltpu.CompilerParams(
            collective_id=0, has_side_effects=True, vmem_limit_bytes=60 * 2**20
        ),
        name="moba",
    )(chosen.T, query_rows, key_rows, value_rows, grad_out)
    return pl.pallas_call(
        finish,
        out_shape=(wide, wide, thin, thin),
        in_specs=[anywhere] * 6,
        out_specs=(anywhere,) * 4,
        scratch_shapes=[
            pltpu.VMEM((2, 1, rows, query_rows.shape[1]), BF16),
            pltpu.VMEM((2, *key_rows.shape), F32),
            pltpu.VMEM((2, *key_rows.shape), BF16),
            pltpu.VMEM((2, *key_rows.shape), BF16),
            pltpu.SemaphoreType.DMA((2, 4)),
            pltpu.SemaphoreType.DMA((2,)),
            pltpu.SemaphoreType.DMA((2,)),
            pltpu.SemaphoreType.DMA((2, 4)),
            pltpu.SemaphoreType.DMA((2,)),
        ],
        name="finish",
    )(*results)


def solution(mesh):
    return jax.shard_map(
        shards,
        mesh=mesh,
        in_specs=(P("ctx", "kvh"), P("ctx", "kvh"), P("ctx", "kvh"), P("ctx", "kvh"), P()),
        out_specs=(P("ctx", "kvh"), P("ctx", "kvh"), P("ctx", "kvh"), P("ctx", "kvh")),
        check_vma=False,
    )
```

```python
import functools
import math

import jax
import jax.numpy as jnp
from jax import lax
from jax.experimental import pallas as pl
from jax.experimental.pallas import tpu as pltpu
from jax.sharding import PartitionSpec as P

HEADS = 32
HEAD_DIM = 128
EPSILON = 1e-06
SCALE = 1.0 / math.sqrt(HEAD_DIM)
SCALE2 = SCALE * math.log2(math.e)
MESH = pl.DeviceIdType.MESH
F32 = jnp.float32
BF16 = jnp.bfloat16
NEG = -jnp.inf


def dot(left, right):
    return jnp.dot(left, right, preferred_element_type=F32)


def aligned(start, size, step):
    return pl.ds(pl.multiple_of(start, step), size)


def kernel(
    blocks, rows, group, kvh,
    chosen, q_in, k_in, v_in, g_in,
    normed_out, gq_out, part_k, part_v, home_k, home_v,
    qs, gos, ks, vs, vtx, kt, qh, qt, gt, held_k, held_v, picked_k, picked_v, probs, maxes, parts,
    weights, att_wide, stat_send, stat_recv, gat, ga, delta, dscores, dk, dv, dk_send, dv_send,
    arrived_k, arrived_v, table, totals_k, totals_v, nrm, gq,
    local_sem, swap_send, swap_recv, hop_send, hop_recv, stat_sems, out_local, out_send, out_recv,
):
    hd = HEAD_DIM
    block = 2 * rows
    piece = block // blocks
    width = group * hd
    ctx = lax.axis_index("ctx")
    y = lax.axis_index("kvh")
    mine = ctx // 2
    core = lax.rem(ctx, 2)
    other = 1 - core
    partner = (2 * mine + other, y)
    far = 2 * (kvh - 1)
    half_blocks = blocks // 2
    upper = mine // half_blocks

    def peer(step):
        return lax.rem(mine + step, blocks)

    def far_member(step):
        return (2 * mine + lax.rem(step, 2), lax.rem(y + 1 + step // 2, kvh))

    def drain(ref, sem):
        pltpu.make_async_copy(ref, ref, sem).wait()

    def send(src, dst, send_sem, recv_sem, device):
        pltpu.make_async_remote_copy(
            src_ref=src, dst_ref=dst, send_sem=send_sem, recv_sem=recv_sem,
            device_id=device, device_id_type=MESH,
        ).start()

    def signal(device):
        pl.semaphore_signal(barrier, inc=1, device_id=device, device_id_type=MESH)

    own_rows = aligned(core * rows, rows, rows)
    other_rows = aligned(other * rows, rows, rows)
    own_head = aligned(core * hd, hd, hd)
    other_head = aligned(other * hd, hd, hd)
    own_group = aligned(core * width, width, width)
    other_group = aligned(other * width, width, width)
    my_piece = aligned(piece * mine, piece, piece)

    fetches = [
        pltpu.make_async_copy(k_in.at[:, own_head], ks.at[0, own_rows, :], local_sem.at[0]),
        pltpu.make_async_copy(v_in.at[:, own_head], vs.at[0, own_rows, :], local_sem.at[1]),
        pltpu.make_async_copy(q_in.at[:, own_group], qs.at[own_rows, :], local_sem.at[2]),
        pltpu.make_async_copy(g_in.at[:, own_group], gos.at[own_rows, :], local_sem.at[3]),
    ]
    for fetch in fetches:
        fetch.start()

    barrier = pltpu.get_barrier_semaphore()

    @pl.loop(1, 2 * blocks)
    def _(step):
        signal((lax.rem(ctx + step, 2 * blocks), y))

    @pl.loop(0, far)
    def _(step):
        signal(far_member(step))

    pl.semaphore_wait(barrier, 2 * blocks - 1 + far)

    swaps = [
        (k_in.at[:, other_head], ks.at[0, own_rows, :]),
        (v_in.at[:, other_head], vs.at[0, own_rows, :]),
        (q_in.at[:, other_group], qs.at[own_rows, :]),
        (g_in.at[:, other_group], gos.at[own_rows, :]),
    ]

    def swap(number):
        src, dst = swaps[number]
        send(src, dst, swap_send.at[number], swap_recv.at[number], partner)

    swap(0)
    swap(1)

    def scatter(number, source, held):
        def scatter_half(half):
            @pl.loop(0, half_blocks)
            def _(step):
                to = half * half_blocks + lax.rem(step + mine, half_blocks)

                @pl.when(to != mine)
                def _():
                    send(
                        source.at[0, aligned(piece * to, piece, piece), :], held.at[mine],
                        hop_send.at[number], hop_recv.at[number], (2 * to + core, y),
                    )

        fetches[number].wait()
        scatter_half(core)
        drain(source.at[0, other_rows, :], swap_recv.at[number])
        scatter_half(other)
        held[mine] = source[0, my_piece, :]

    scatter(0, ks, held_k)
    drain(held_k.at[pl.ds(0, blocks - 1)], hop_send.at[0])
    scatter(1, vs, held_v)
    swap(2)
    swap(3)

    for number, target in ((2, qs), (3, gos)):
        fetches[number].wait()
        drain(target.at[other_rows, :], swap_recv.at[number])

    def turn_keys(section):
        kt[:, section * block : (section + 1) * block] = ks[section].T

    def turn_values(section):
        vtx[section, 0:hd, :] = vs[section].T
        vtx[section, hd : hd + 16, :] = jnp.ones((16, block), BF16)

    def head_lanes(head):
        return aligned(head * block, block, block)

    def score(section, head):
        scores = dot(ks[section], qt[head])
        if section == 0:
            key_at = lax.broadcasted_iota(jnp.int32, (block, block), 0)
            row_at = lax.broadcasted_iota(jnp.int32, (block, block), 1)
            key_order = 2 * lax.rem(key_at, rows) + key_at // rows
            row_order = 2 * lax.rem(row_at, rows) + row_at // rows
            scores = jnp.where(key_order <= row_order, scores, NEG)
        top = jnp.max(scores, axis=0, keepdims=True)
        terms = jnp.exp2((scores - top) * SCALE2).astype(BF16)
        probs[section, :, head_lanes(head)] = terms
        maxes[section, head] = jnp.broadcast_to(top, (8, block))
        return terms

    def deliver_keys():
        drain(held_k.at[pl.ds(0, blocks - 1)], hop_recv.at[0])

        @pl.loop(1, blocks)
        def _(step):
            to = peer(step)
            for pick in range(2):
                picked_k[to, pick] = held_k[chosen[pick, to]]
            send(
                picked_k.at[to], ks.at[pl.ds(1, 2), my_piece, :],
                hop_send.at[2], hop_recv.at[2], (2 * to + core, y),
            )

        for pick in range(2):
            ks[1 + pick, my_piece, :] = held_k[chosen[pick, mine]]

    def deliver_values(pick):
        @pl.loop(1, blocks)
        def _(step):
            to = peer(step)
            picked_v[pick, to] = held_v[chosen[pick, to]]
            send(
                picked_v.at[pick, to], vs.at[1 + pick, my_piece, :],
                hop_send.at[3 + pick], hop_recv.at[3 + pick], (2 * to + core, y),
            )

        vs[1 + pick, my_piece, :] = held_v[chosen[pick, mine]]

    turn_keys(0)

    @pl.loop(0, group, unroll=2)
    def _(head):
        queries = qs[:, aligned(head * hd, hd, hd)]
        qh[aligned(head * block, block, block), :] = queries
        qt[head] = queries.T

    drain(held_v.at[pl.ds(0, blocks - 1)], hop_send.at[1])
    deliver_keys()
    turn_values(0)

    @pl.loop(0, group, unroll=2)
    def _(head):
        gt[head] = gos[:, aligned(head * hd, hd, hd)].T

    @pl.loop(0, group, unroll=2)
    def _(head):
        parts[0, head] = dot(vtx[0], score(0, head))

    drain(held_v.at[pl.ds(0, blocks - 1)], hop_recv.at[1])
    deliver_values(0)

    for pick in range(2):
        lane_owner = lax.broadcasted_iota(jnp.int32, (8, block), 1) // piece

        def fill(reader, owners):
            choice = chosen[pick, reader]
            choice = jnp.where(choice < reader, choice, -1)
            return jnp.where(lane_owner == reader, choice, owners)

        owners = lax.fori_loop(0, blocks, fill, jnp.full((8, block), -1, jnp.int32))
        row_at = lax.broadcasted_iota(jnp.int32, (block, block), 0)
        lane_at = lax.broadcasted_iota(jnp.int32, (block, block), 1)
        wanted = owners[0:1] * piece + lax.rem(lane_at, piece)
        table[pick] = (row_at == wanted).astype(F32).astype(BF16)

    deliver_values(1)
    drain(ks.at[pl.ds(1, 2), pl.ds(0, block - piece), :], hop_recv.at[2])
    for pick in range(2):
        @pl.loop(0, group, unroll=2)
        def _(head):
            score(1 + pick, head)

        turn_keys(1 + pick)

    for pick in range(2):
        drain(vs.at[1 + pick, pl.ds(0, block - piece), :], hop_recv.at[3 + pick])
        turn_values(1 + pick)

        @pl.loop(0, group, unroll=2)
        def _(head):
            parts[1 + pick, head] = dot(vtx[1 + pick], probs[1 + pick, :, head_lanes(head)])

    valid = [chosen[pick, mine] < mine for pick in range(2)]

    def merge(head, sums):
        top_own = maxes[0, head, 0:1]
        tops = [top_own] + [
            jnp.where(valid[pick], maxes[1 + pick, head, 0:1], NEG) for pick in range(2)
        ]
        top = jnp.maximum(jnp.maximum(tops[0], tops[1]), tops[2])
        ratios = [jnp.exp2((value - top) * SCALE2) for value in tops]
        total = sum(
            ratio * parts[section, head, hd : hd + 1] for section, ratio in enumerate(ratios)
        )
        inverse = 1.0 / total
        shares = [ratio * inverse for ratio in ratios]
        for section in range(3):
            weights[section, head] = jnp.broadcast_to(shares[section], (8, block))
        wide = sum(share * parts[section, head, 0:hd] for section, share in enumerate(shares))
        att_wide[head] = wide
        rounded = wide.astype(BF16).astype(F32)
        upstream = gt[head].astype(F32)
        return (
            sums[0] + jnp.sum(rounded * rounded, axis=0, keepdims=True),
            sums[1] + jnp.sum(rounded * upstream, axis=0, keepdims=True),
        )

    zero_row = jnp.zeros((1, block), F32)
    square_sum, cross_sum = lax.fori_loop(0, group, merge, (zero_row, zero_row))
    folds = block // 128
    stat_send[...] = jnp.concatenate(
        [
            total[:, at * 128 : (at + 1) * 128]
            for total in (square_sum, cross_sum)
            for at in range(folds)
        ],
        axis=0,
    )
    slot = 2 * y + core
    send(stat_send, stat_recv.at[slot], stat_sems.at[0], stat_sems.at[1], partner)

    @pl.loop(0, far)
    def _(step):
        send(stat_send, stat_recv.at[slot], stat_sems.at[0], stat_sems.at[1], far_member(step))

    stat_recv[slot] = stat_send[...]

    @pl.loop(0, group, unroll=2)
    def _(head):
        lanes = head_lanes(head)
        for section in range(3):
            share = probs[section, :, lanes].astype(F32) * weights[section, head, 0:1]
            probs[section, :, lanes] = share.astype(BF16)

    drain(stat_recv.at[pl.ds(0, far + 1)], stat_sems.at[1])
    stats = stat_recv[0]
    for at in range(1, far + 2):
        stats = stats + stat_recv[at]
    features = HEADS * HEAD_DIM
    square_row = jnp.concatenate([stats[at : at + 1] for at in range(folds)], axis=1)
    cross_row = jnp.concatenate([stats[folds + at : folds + at + 1] for at in range(folds)], axis=1)
    rscale = lax.rsqrt(square_row / features + EPSILON)
    factor = rscale * rscale * rscale * (cross_row / features)

    @pl.loop(0, group, unroll=2)
    def _(head):
        wide = att_wide[head]
        rounded = wide.astype(BF16).astype(F32)
        upstream = gt[head].astype(F32)
        grad = (rscale * upstream - rounded * factor).astype(BF16)
        gat[head] = grad
        ga[head_lanes(head), :] = grad.T
        delta[head] = jnp.broadcast_to(
            jnp.sum(wide * grad.astype(F32), axis=0, keepdims=True), (8, block)
        )

    def value_grad(section):
        return dot(probs[section], ga[...])

    def key_grad(section):
        @pl.loop(0, group, unroll=2)
        def _(head):
            lanes = head_lanes(head)
            dprob = dot(vs[section], gat[head])
            share = probs[section, :, lanes].astype(F32)
            dscore = (share * (dprob - delta[head, 0:1])).astype(BF16)
            dscores[section * block : (section + 1) * block, lanes] = dscore

        return dot(dscores[section * block : (section + 1) * block, :], qh[...]) * SCALE

    def give_back(number, pick, source, arrived):
        @pl.loop(1, blocks)
        def _(step):
            to = peer(step)
            send(
                source.at[pick, aligned(piece * to, piece, piece), :],
                arrived.at[pick, my_piece, :],
                hop_send.at[number], hop_recv.at[number], (2 * to + core, y),
            )

        arrived[pick, my_piece, :] = source[pick, my_piece, :]

    for pick in range(2):
        dv_send[pick] = value_grad(1 + pick).astype(BF16)
        give_back(5 + pick, pick, dv_send, arrived_v)
    for pick in range(2):
        dk_send[pick] = key_grad(1 + pick).astype(BF16)
        give_back(7 + pick, pick, dk_send, arrived_k)

    def hand_out(number, buffer, out, lanes):
        send(
            buffer.at[other_rows, :], out.at[:, lanes],
            out_send.at[number], out_recv.at[number], partner,
        )
        keep = pltpu.make_async_copy(
            buffer.at[own_rows, :], out.at[:, lanes], out_local.at[number]
        )
        keep.start()
        return keep

    def settle(number, arrival, arrived, totals, home):
        for pick in range(2):
            drain(arrived.at[pick, pl.ds(0, block - piece), :], hop_recv.at[arrival + pick])
        totals[...] = (dot(table[0], arrived[0]) + dot(table[1], arrived[1])).astype(BF16)
        target = home.at[aligned(piece * lax.rem(mine, half_blocks), piece, piece), own_head]

        @pl.loop(1, blocks)
        def _(step):
            to = peer(step)
            send(
                totals.at[aligned(piece * to, piece, piece), :], target,
                hop_send.at[number], hop_recv.at[number], (2 * to + upper, y),
            )

        @pl.when(upper != core)
        def _():
            send(
                totals.at[my_piece, :], target,
                hop_send.at[number], hop_recv.at[number], partner,
            )

        @pl.when(upper == core)
        def _():
            pltpu.make_async_copy(totals.at[my_piece, :], target, hop_recv.at[number]).start()

    dv[...] = value_grad(0)
    keeps = [hand_out(0, dv, part_v, own_head)]
    dk[...] = key_grad(0)
    keeps.append(hand_out(1, dk, part_k, own_head))
    settle(9, 5, arrived_v, totals_v, home_v)

    @pl.loop(0, group, unroll=2)
    def _(head):
        lanes = aligned(head * hd, hd, hd)
        grad = dot(kt[...], dscores[:, head_lanes(head)]) * SCALE
        gq[:, lanes] = grad.astype(BF16).T


    @pl.loop(0, group, unroll=2)
    def _(head):
        lanes = aligned(head * hd, hd, hd)
        nrm[:, lanes] = (att_wide[head].astype(BF16).astype(F32) * rscale).astype(BF16).T

    settle(10, 7, arrived_k, totals_k, home_k)
    keeps.append(hand_out(2, gq, gq_out, own_group))
    keeps.append(hand_out(3, nrm, normed_out, own_group))

    for number, (src, _) in enumerate(swaps):
        drain(src, swap_send.at[number])
    drain(picked_v.at[1, pl.ds(0, blocks - 1)], hop_send.at[4])
    drain(picked_k.at[pl.ds(0, blocks - 1)], hop_send.at[2])
    drain(picked_v.at[0, pl.ds(0, blocks - 1)], hop_send.at[3])
    for number, buffer in ((5, dv_send), (7, dk_send)):
        for pick in range(2):
            drain(buffer.at[pick, pl.ds(0, block - piece), :], hop_send.at[number + pick])
    drain(stat_recv.at[pl.ds(0, far + 1)], stat_sems.at[0])
    for keep in keeps:
        keep.wait()
    for number, (buffer, out, lanes) in enumerate((
        (dv, part_v, other_head), (dk, part_k, other_head),
        (gq, gq_out, other_group), (nrm, normed_out, other_group),
    )):
        drain(buffer.at[other_rows, :], out_send.at[number])
        drain(out.at[:, lanes], out_recv.at[number])
    for number in (9, 10):
        drain(totals_k.at[pl.ds(0, block - piece), :], hop_send.at[number])

        @pl.when(upper != core)
        def _():
            drain(totals_k.at[my_piece, :], hop_send.at[number])

    drain(home_v, hop_recv.at[9])
    drain(home_k, hop_recv.at[10])


def finish(
    normed_in, gq_in, part_k, part_v, home_k, home_v,
    normed_out, gq_out, gk_out, gv_out,
    wides, parts, homes, grads, in_sems, part_sems, home_sems, out_sems, grad_sems,
):
    chunks = wides.shape[1]
    rows = wides.shape[2]
    loads = []
    stores = []
    for number, (src, dst) in enumerate(((normed_in, normed_out), (gq_in, gq_out))):
        for at in range(chunks):
            span = pl.ds(at * rows, rows)
            held = wides.at[number, at]
            loads.append(pltpu.make_async_copy(src.at[span, :], held, in_sems.at[number, at]))
            stores.append(pltpu.make_async_copy(held, dst.at[span, :], out_sems.at[number, at]))
    terms = []
    for number, (part, home) in enumerate(((part_k, home_k), (part_v, home_v))):
        terms.append((
            pltpu.make_async_copy(part, parts.at[number], part_sems.at[number]),
            pltpu.make_async_copy(home, homes.at[number], home_sems.at[number]),
        ))
    for load in loads:
        load.start()
    for part_load, home_load in terms:
        part_load.start()
        home_load.start()
    for load, store in zip(loads, stores):
        load.wait()
        store.start()
    for number, out in enumerate((gk_out, gv_out)):
        terms[number][0].wait()
        terms[number][1].wait()
        grads[number] = (parts[number] + homes[number].astype(F32)).astype(BF16)
        store = pltpu.make_async_copy(grads.at[number], out, grad_sems.at[number])
        store.start()
        stores.append(store)
    for store in stores:
        store.wait()


def shards(query_rows, key_rows, value_rows, grad_out, chosen):
    blocks = chosen.shape[0]
    rows, kv_width = key_rows.shape
    group = query_rows.shape[1] // kv_width
    kvh = lax.axis_size("kvh")
    hd = HEAD_DIM
    block = 2 * rows
    piece = block // blocks
    width = group * hd
    anywhere = pl.BlockSpec(memory_space=pl.ANY)
    scratch = [
        pltpu.VMEM((block, width), BF16),
        pltpu.VMEM((block, width), BF16),
        pltpu.VMEM((3, block, hd), BF16),
        pltpu.VMEM((3, block, hd), BF16),
        pltpu.VMEM((3, hd + 16, block), BF16),
        pltpu.VMEM((hd, 3 * block), BF16),
        pltpu.VMEM((group * block, hd), BF16),
        pltpu.VMEM((group, hd, block), BF16),
        pltpu.VMEM((group, hd, block), BF16),
        pltpu.VMEM((blocks, piece, hd), BF16),
        pltpu.VMEM((blocks, piece, hd), BF16),
        pltpu.VMEM((blocks, 2, piece, hd), BF16),
        pltpu.VMEM((2, blocks, piece, hd), BF16),
        pltpu.VMEM((3, block, group * block), BF16),
        pltpu.VMEM((3, group, 8, block), F32),
        pltpu.VMEM((3, group, hd + 16, block), F32),
        pltpu.VMEM((3, group, 8, block), F32),
        pltpu.VMEM((group, hd, block), F32),
        pltpu.VMEM((2 * block // 128, 128), F32),
        pltpu.VMEM((2 * kvh, 2 * block // 128, 128), F32),
        pltpu.VMEM((group, hd, block), BF16),
        pltpu.VMEM((group * block, hd), BF16),
        pltpu.VMEM((group, 8, block), F32),
        pltpu.VMEM((3 * block, group * block), BF16),
        pltpu.VMEM((block, hd), F32),
        pltpu.VMEM((block, hd), F32),
        pltpu.VMEM((2, block, hd), BF16),
        pltpu.VMEM((2, block, hd), BF16),
        pltpu.VMEM((2, block, hd), BF16),
        pltpu.VMEM((2, block, hd), BF16),
        pltpu.VMEM((2, block, block), BF16),
        pltpu.VMEM((block, hd), BF16),
        pltpu.VMEM((block, hd), BF16),
        pltpu.VMEM((block, width), BF16),
        pltpu.VMEM((block, width), BF16),
        pltpu.SemaphoreType.DMA((4,)),
        pltpu.SemaphoreType.DMA((4,)),
        pltpu.SemaphoreType.DMA((4,)),
        pltpu.SemaphoreType.DMA((11,)),
        pltpu.SemaphoreType.DMA((11,)),
        pltpu.SemaphoreType.DMA((2,)),
        pltpu.SemaphoreType.DMA((4,)),
        pltpu.SemaphoreType.DMA((4,)),
        pltpu.SemaphoreType.DMA((4,)),
    ]
    wide = jax.ShapeDtypeStruct(query_rows.shape, BF16)
    part = jax.ShapeDtypeStruct(key_rows.shape, F32)
    thin = jax.ShapeDtypeStruct(key_rows.shape, BF16)
    results = pl.pallas_call(
        functools.partial(kernel, blocks, rows, group, kvh),
        out_shape=(wide, wide, part, part, thin, thin),
        in_specs=[pl.BlockSpec(memory_space=pltpu.SMEM)] + [anywhere] * 4,
        out_specs=(anywhere,) * 6,
        scratch_shapes=scratch,
        compiler_params=pltpu.CompilerParams(
            collective_id=0, has_side_effects=True, vmem_limit_bytes=60 * 2**20
        ),
        name="moba",
    )(chosen.T, query_rows, key_rows, value_rows, grad_out)
    return pl.pallas_call(
        finish,
        out_shape=(wide, wide, thin, thin),
        in_specs=[anywhere] * 6,
        out_specs=(anywhere,) * 4,
        scratch_shapes=[
            pltpu.VMEM((2, 1, rows, query_rows.shape[1]), BF16),
            pltpu.VMEM((2, *key_rows.shape), F32),
            pltpu.VMEM((2, *key_rows.shape), BF16),
            pltpu.VMEM((2, *key_rows.shape), BF16),
            pltpu.SemaphoreType.DMA((2, 4)),
            pltpu.SemaphoreType.DMA((2,)),
            pltpu.SemaphoreType.DMA((2,)),
            pltpu.SemaphoreType.DMA((2, 4)),
            pltpu.SemaphoreType.DMA((2,)),
        ],
        name="finish",
    )(*results)


def solution(mesh):
    return jax.shard_map(
        shards,
        mesh=mesh,
        in_specs=(P("ctx", "kvh"), P("ctx", "kvh"), P("ctx", "kvh"), P("ctx", "kvh"), P()),
        out_specs=(P("ctx", "kvh"), P("ctx", "kvh"), P("ctx", "kvh"), P("ctx", "kvh")),
        check_vma=False,
    )
```

```python
import functools
import math

import jax
import jax.numpy as jnp
from jax import lax
from jax.experimental import pallas as pl
from jax.experimental.pallas import tpu as pltpu
from jax.sharding import PartitionSpec as P

HEADS = 32
HEAD_DIM = 128
EPSILON = 1e-06
SCALE = 1.0 / math.sqrt(HEAD_DIM)
SCALE2 = SCALE * math.log2(math.e)
MESH = pl.DeviceIdType.MESH
F32 = jnp.float32
BF16 = jnp.bfloat16
NEG = -jnp.inf


def dot(left, right):
    return jnp.dot(left, right, preferred_element_type=F32)


def aligned(start, size, step):
    return pl.ds(pl.multiple_of(start, step), size)


def kernel(
    blocks, rows, group, kvh,
    chosen, q_in, k_in, v_in, g_in,
    normed_out, gq_out, part_k, part_v, home_k, home_v,
    qs, gos, ks, vs, vtx, kt, qh, qt, gt, held_k, held_v, picked_k, picked_v, probs, maxes, parts,
    weights, att_wide, stat_send, stat_recv, gat, ga, delta, dscores, dk, dv, dk_send, dv_send,
    arrived_k, arrived_v, table, totals_k, totals_v, nrm, gq,
    local_sem, swap_send, swap_recv, hop_send, hop_recv, stat_sems, out_local, out_send, out_recv,
):
    hd = HEAD_DIM
    block = 2 * rows
    piece = block // blocks
    width = group * hd
    ctx = lax.axis_index("ctx")
    y = lax.axis_index("kvh")
    mine = ctx // 2
    core = lax.rem(ctx, 2)
    other = 1 - core
    partner = (2 * mine + other, y)
    far = 2 * (kvh - 1)
    half_blocks = blocks // 2
    upper = mine // half_blocks

    def peer(step):
        return lax.rem(mine + step, blocks)

    def far_member(step):
        return (2 * mine + lax.rem(step, 2), lax.rem(y + 1 + step // 2, kvh))

    def drain(ref, sem):
        pltpu.make_async_copy(ref, ref, sem).wait()

    def send(src, dst, send_sem, recv_sem, device):
        pltpu.make_async_remote_copy(
            src_ref=src, dst_ref=dst, send_sem=send_sem, recv_sem=recv_sem,
            device_id=device, device_id_type=MESH,
        ).start()

    def signal(device):
        pl.semaphore_signal(barrier, inc=1, device_id=device, device_id_type=MESH)

    own_rows = aligned(core * rows, rows, rows)
    other_rows = aligned(other * rows, rows, rows)
    own_head = aligned(core * hd, hd, hd)
    other_head = aligned(other * hd, hd, hd)
    own_group = aligned(core * width, width, width)
    other_group = aligned(other * width, width, width)
    my_piece = aligned(piece * mine, piece, piece)

    fetches = [
        pltpu.make_async_copy(k_in.at[:, own_head], ks.at[0, own_rows, :], local_sem.at[0]),
        pltpu.make_async_copy(v_in.at[:, own_head], vs.at[0, own_rows, :], local_sem.at[1]),
        pltpu.make_async_copy(q_in.at[:, own_group], qs.at[own_rows, :], local_sem.at[2]),
        pltpu.make_async_copy(g_in.at[:, own_group], gos.at[own_rows, :], local_sem.at[3]),
    ]
    for fetch in fetches:
        fetch.start()

    barrier = pltpu.get_barrier_semaphore()

    @pl.loop(1, 2 * blocks)
    def _(step):
        signal((lax.rem(ctx + step, 2 * blocks), y))

    @pl.loop(0, far)
    def _(step):
        signal(far_member(step))

    pl.semaphore_wait(barrier, 2 * blocks - 1 + far)

    swaps = [
        (k_in.at[:, other_head], ks.at[0, own_rows, :]),
        (v_in.at[:, other_head], vs.at[0, own_rows, :]),
        (q_in.at[:, other_group], qs.at[own_rows, :]),
        (g_in.at[:, other_group], gos.at[own_rows, :]),
    ]

    def swap(number):
        src, dst = swaps[number]
        send(src, dst, swap_send.at[number], swap_recv.at[number], partner)

    swap(0)
    swap(1)

    def scatter(number, source, held):
        def scatter_half(half):
            @pl.loop(0, half_blocks)
            def _(step):
                to = half * half_blocks + lax.rem(step + mine, half_blocks)

                @pl.when(to != mine)
                def _():
                    send(
                        source.at[0, aligned(piece * to, piece, piece), :], held.at[mine],
                        hop_send.at[number], hop_recv.at[number], (2 * to + core, y),
                    )

        fetches[number].wait()
        scatter_half(core)
        drain(source.at[0, other_rows, :], swap_recv.at[number])
        scatter_half(other)
        held[mine] = source[0, my_piece, :]

    scatter(0, ks, held_k)
    drain(held_k.at[pl.ds(0, blocks - 1)], hop_send.at[0])
    scatter(1, vs, held_v)
    swap(2)
    swap(3)

    for number, target in ((2, qs), (3, gos)):
        fetches[number].wait()
        drain(target.at[other_rows, :], swap_recv.at[number])

    def turn_keys(section):
        kt[:, section * block : (section + 1) * block] = ks[section].T

    def turn_values(section):
        vtx[section, 0:hd, :] = vs[section].T
        vtx[section, hd : hd + 16, :] = jnp.ones((16, block), BF16)

    def head_lanes(head):
        return aligned(head * block, block, block)

    def score(section, head):
        scores = dot(ks[section], qt[head])
        if section == 0:
            key_at = lax.broadcasted_iota(jnp.int32, (block, block), 0)
            row_at = lax.broadcasted_iota(jnp.int32, (block, block), 1)
            key_order = 2 * lax.rem(key_at, rows) + key_at // rows
            row_order = 2 * lax.rem(row_at, rows) + row_at // rows
            scores = jnp.where(key_order <= row_order, scores, NEG)
        top = jnp.max(scores, axis=0, keepdims=True)
        terms = jnp.exp2((scores - top) * SCALE2).astype(BF16)
        probs[section, :, head_lanes(head)] = terms
        maxes[section, head] = jnp.broadcast_to(top, (8, block))
        return terms

    def deliver_keys():
        drain(held_k.at[pl.ds(0, blocks - 1)], hop_recv.at[0])

        @pl.loop(1, blocks)
        def _(step):
            to = peer(step)
            for pick in range(2):
                picked_k[to, pick] = held_k[chosen[pick, to]]
            send(
                picked_k.at[to], ks.at[pl.ds(1, 2), my_piece, :],
                hop_send.at[2], hop_recv.at[2], (2 * to + core, y),
            )

        for pick in range(2):
            ks[1 + pick, my_piece, :] = held_k[chosen[pick, mine]]

    def deliver_values(pick):
        @pl.loop(1, blocks)
        def _(step):
            to = peer(step)
            picked_v[pick, to] = held_v[chosen[pick, to]]
            send(
                picked_v.at[pick, to], vs.at[1 + pick, my_piece, :],
                hop_send.at[3 + pick], hop_recv.at[3 + pick], (2 * to + core, y),
            )

        vs[1 + pick, my_piece, :] = held_v[chosen[pick, mine]]

    turn_keys(0)

    @pl.loop(0, group, unroll=2)
    def _(head):
        queries = qs[:, aligned(head * hd, hd, hd)]
        qh[aligned(head * block, block, block), :] = queries
        qt[head] = queries.T

    drain(held_v.at[pl.ds(0, blocks - 1)], hop_send.at[1])
    deliver_keys()
    turn_values(0)

    @pl.loop(0, group, unroll=2)
    def _(head):
        gt[head] = gos[:, aligned(head * hd, hd, hd)].T

    @pl.loop(0, group, unroll=2)
    def _(head):
        parts[0, head] = dot(vtx[0], score(0, head))

    drain(held_v.at[pl.ds(0, blocks - 1)], hop_recv.at[1])
    deliver_values(0)

    deliver_values(1)
    drain(ks.at[pl.ds(1, 2), pl.ds(0, block - piece), :], hop_recv.at[2])
    for pick in range(2):
        @pl.loop(0, group, unroll=2)
        def _(head):
            score(1 + pick, head)

        turn_keys(1 + pick)

    for pick in range(2):
        drain(vs.at[1 + pick, pl.ds(0, block - piece), :], hop_recv.at[3 + pick])
        turn_values(1 + pick)

        @pl.loop(0, group, unroll=2)
        def _(head):
            parts[1 + pick, head] = dot(vtx[1 + pick], probs[1 + pick, :, head_lanes(head)])

    valid = [chosen[pick, mine] < mine for pick in range(2)]

    def merge(head, sums):
        top_own = maxes[0, head, 0:1]
        tops = [top_own] + [
            jnp.where(valid[pick], maxes[1 + pick, head, 0:1], NEG) for pick in range(2)
        ]
        top = jnp.maximum(jnp.maximum(tops[0], tops[1]), tops[2])
        ratios = [jnp.exp2((value - top) * SCALE2) for value in tops]
        total = sum(
            ratio * parts[section, head, hd : hd + 1] for section, ratio in enumerate(ratios)
        )
        inverse = 1.0 / total
        shares = [ratio * inverse for ratio in ratios]
        for section in range(3):
            weights[section, head] = jnp.broadcast_to(shares[section], (8, block))
        wide = sum(share * parts[section, head, 0:hd] for section, share in enumerate(shares))
        att_wide[head] = wide
        rounded = wide.astype(BF16).astype(F32)
        upstream = gt[head].astype(F32)
        return (
            sums[0] + jnp.sum(rounded * rounded, axis=0, keepdims=True),
            sums[1] + jnp.sum(rounded * upstream, axis=0, keepdims=True),
        )

    zero_row = jnp.zeros((1, block), F32)
    square_sum, cross_sum = lax.fori_loop(0, group, merge, (zero_row, zero_row))
    folds = block // 128
    stat_send[...] = jnp.concatenate(
        [
            total[:, at * 128 : (at + 1) * 128]
            for total in (square_sum, cross_sum)
            for at in range(folds)
        ],
        axis=0,
    )
    slot = 2 * y + core
    send(stat_send, stat_recv.at[slot], stat_sems.at[0], stat_sems.at[1], partner)

    @pl.loop(0, far)
    def _(step):
        send(stat_send, stat_recv.at[slot], stat_sems.at[0], stat_sems.at[1], far_member(step))

    stat_recv[slot] = stat_send[...]

    @pl.loop(0, group, unroll=2)
    def _(head):
        lanes = head_lanes(head)
        for section in range(3):
            share = probs[section, :, lanes].astype(F32) * weights[section, head, 0:1]
            probs[section, :, lanes] = share.astype(BF16)

    for pick in range(2):
        lane_owner = lax.broadcasted_iota(jnp.int32, (8, block), 1) // piece

        def fill(reader, owners):
            choice = chosen[pick, reader]
            choice = jnp.where(choice < reader, choice, -1)
            return jnp.where(lane_owner == reader, choice, owners)

        owners = lax.fori_loop(0, blocks, fill, jnp.full((8, block), -1, jnp.int32))
        row_at = lax.broadcasted_iota(jnp.int32, (block, block), 0)
        lane_at = lax.broadcasted_iota(jnp.int32, (block, block), 1)
        wanted = owners[0:1] * piece + lax.rem(lane_at, piece)
        table[pick] = (row_at == wanted).astype(F32).astype(BF16)

    drain(stat_recv.at[pl.ds(0, far + 1)], stat_sems.at[1])
    stats = stat_recv[0]
    for at in range(1, far + 2):
        stats = stats + stat_recv[at]
    features = HEADS * HEAD_DIM
    square_row = jnp.concatenate([stats[at : at + 1] for at in range(folds)], axis=1)
    cross_row = jnp.concatenate([stats[folds + at : folds + at + 1] for at in range(folds)], axis=1)
    rscale = lax.rsqrt(square_row / features + EPSILON)
    factor = rscale * rscale * rscale * (cross_row / features)

    @pl.loop(0, group, unroll=2)
    def _(head):
        wide = att_wide[head]
        rounded = wide.astype(BF16).astype(F32)
        upstream = gt[head].astype(F32)
        grad = (rscale * upstream - rounded * factor).astype(BF16)
        gat[head] = grad
        ga[head_lanes(head), :] = grad.T
        delta[head] = jnp.broadcast_to(
            jnp.sum(wide * grad.astype(F32), axis=0, keepdims=True), (8, block)
        )

    def value_grad(section):
        return dot(probs[section], ga[...])

    def key_grad(section):
        @pl.loop(0, group, unroll=2)
        def _(head):
            lanes = head_lanes(head)
            dprob = dot(vs[section], gat[head])
            share = probs[section, :, lanes].astype(F32)
            dscore = (share * (dprob - delta[head, 0:1])).astype(BF16)
            dscores[section * block : (section + 1) * block, lanes] = dscore

        return dot(dscores[section * block : (section + 1) * block, :], qh[...]) * SCALE

    def give_back(number, pick, source, arrived):
        @pl.loop(1, blocks)
        def _(step):
            to = peer(step)
            send(
                source.at[pick, aligned(piece * to, piece, piece), :],
                arrived.at[pick, my_piece, :],
                hop_send.at[number], hop_recv.at[number], (2 * to + core, y),
            )

        arrived[pick, my_piece, :] = source[pick, my_piece, :]

    for pick in range(2):
        dv_send[pick] = value_grad(1 + pick).astype(BF16)
        give_back(5 + pick, pick, dv_send, arrived_v)
    for pick in range(2):
        dk_send[pick] = key_grad(1 + pick).astype(BF16)
        give_back(7 + pick, pick, dk_send, arrived_k)

    def hand_out(number, buffer, out, lanes):
        send(
            buffer.at[other_rows, :], out.at[:, lanes],
            out_send.at[number], out_recv.at[number], partner,
        )
        keep = pltpu.make_async_copy(
            buffer.at[own_rows, :], out.at[:, lanes], out_local.at[number]
        )
        keep.start()
        return keep

    def settle(number, arrival, arrived, totals, home):
        for pick in range(2):
            drain(arrived.at[pick, pl.ds(0, block - piece), :], hop_recv.at[arrival + pick])
        totals[...] = (dot(table[0], arrived[0]) + dot(table[1], arrived[1])).astype(BF16)
        target = home.at[aligned(piece * lax.rem(mine, half_blocks), piece, piece), own_head]

        @pl.loop(1, blocks)
        def _(step):
            to = peer(step)
            send(
                totals.at[aligned(piece * to, piece, piece), :], target,
                hop_send.at[number], hop_recv.at[number], (2 * to + upper, y),
            )

        @pl.when(upper != core)
        def _():
            send(
                totals.at[my_piece, :], target,
                hop_send.at[number], hop_recv.at[number], partner,
            )

        @pl.when(upper == core)
        def _():
            pltpu.make_async_copy(totals.at[my_piece, :], target, hop_recv.at[number]).start()

    dv[...] = value_grad(0)
    keeps = [hand_out(0, dv, part_v, own_head)]
    dk[...] = key_grad(0)
    keeps.append(hand_out(1, dk, part_k, own_head))
    settle(9, 5, arrived_v, totals_v, home_v)

    @pl.loop(0, group, unroll=2)
    def _(head):
        lanes = aligned(head * hd, hd, hd)
        grad = dot(kt[...], dscores[:, head_lanes(head)]) * SCALE
        gq[:, lanes] = grad.astype(BF16).T


    @pl.loop(0, group, unroll=2)
    def _(head):
        lanes = aligned(head * hd, hd, hd)
        nrm[:, lanes] = (att_wide[head].astype(BF16).astype(F32) * rscale).astype(BF16).T

    settle(10, 7, arrived_k, totals_k, home_k)
    keeps.append(hand_out(2, gq, gq_out, own_group))
    keeps.append(hand_out(3, nrm, normed_out, own_group))

    for number, (src, _) in enumerate(swaps):
        drain(src, swap_send.at[number])
    drain(picked_v.at[1, pl.ds(0, blocks - 1)], hop_send.at[4])
    drain(picked_k.at[pl.ds(0, blocks - 1)], hop_send.at[2])
    drain(picked_v.at[0, pl.ds(0, blocks - 1)], hop_send.at[3])
    for number, buffer in ((5, dv_send), (7, dk_send)):
        for pick in range(2):
            drain(buffer.at[pick, pl.ds(0, block - piece), :], hop_send.at[number + pick])
    drain(stat_recv.at[pl.ds(0, far + 1)], stat_sems.at[0])
    for keep in keeps:
        keep.wait()
    for number, (buffer, out, lanes) in enumerate((
        (dv, part_v, other_head), (dk, part_k, other_head),
        (gq, gq_out, other_group), (nrm, normed_out, other_group),
    )):
        drain(buffer.at[other_rows, :], out_send.at[number])
        drain(out.at[:, lanes], out_recv.at[number])
    for number in (9, 10):
        drain(totals_k.at[pl.ds(0, block - piece), :], hop_send.at[number])

        @pl.when(upper != core)
        def _():
            drain(totals_k.at[my_piece, :], hop_send.at[number])

    drain(home_v, hop_recv.at[9])
    drain(home_k, hop_recv.at[10])


def finish(
    normed_in, gq_in, part_k, part_v, home_k, home_v,
    normed_out, gq_out, gk_out, gv_out,
    wides, parts, homes, grads, in_sems, part_sems, home_sems, out_sems, grad_sems,
):
    chunks = wides.shape[1]
    rows = wides.shape[2]
    loads = []
    stores = []
    for number, (src, dst) in enumerate(((normed_in, normed_out), (gq_in, gq_out))):
        for at in range(chunks):
            span = pl.ds(at * rows, rows)
            held = wides.at[number, at]
            loads.append(pltpu.make_async_copy(src.at[span, :], held, in_sems.at[number, at]))
            stores.append(pltpu.make_async_copy(held, dst.at[span, :], out_sems.at[number, at]))
    terms = []
    for number, (part, home) in enumerate(((part_k, home_k), (part_v, home_v))):
        terms.append((
            pltpu.make_async_copy(part, parts.at[number], part_sems.at[number]),
            pltpu.make_async_copy(home, homes.at[number], home_sems.at[number]),
        ))
    for load in loads:
        load.start()
    for part_load, home_load in terms:
        part_load.start()
        home_load.start()
    for load, store in zip(loads, stores):
        load.wait()
        store.start()
    for number, out in enumerate((gk_out, gv_out)):
        terms[number][0].wait()
        terms[number][1].wait()
        grads[number] = (parts[number] + homes[number].astype(F32)).astype(BF16)
        store = pltpu.make_async_copy(grads.at[number], out, grad_sems.at[number])
        store.start()
        stores.append(store)
    for store in stores:
        store.wait()


def shards(query_rows, key_rows, value_rows, grad_out, chosen):
    blocks = chosen.shape[0]
    rows, kv_width = key_rows.shape
    group = query_rows.shape[1] // kv_width
    kvh = lax.axis_size("kvh")
    hd = HEAD_DIM
    block = 2 * rows
    piece = block // blocks
    width = group * hd
    anywhere = pl.BlockSpec(memory_space=pl.ANY)
    scratch = [
        pltpu.VMEM((block, width), BF16),
        pltpu.VMEM((block, width), BF16),
        pltpu.VMEM((3, block, hd), BF16),
        pltpu.VMEM((3, block, hd), BF16),
        pltpu.VMEM((3, hd + 16, block), BF16),
        pltpu.VMEM((hd, 3 * block), BF16),
        pltpu.VMEM((group * block, hd), BF16),
        pltpu.VMEM((group, hd, block), BF16),
        pltpu.VMEM((group, hd, block), BF16),
        pltpu.VMEM((blocks, piece, hd), BF16),
        pltpu.VMEM((blocks, piece, hd), BF16),
        pltpu.VMEM((blocks, 2, piece, hd), BF16),
        pltpu.VMEM((2, blocks, piece, hd), BF16),
        pltpu.VMEM((3, block, group * block), BF16),
        pltpu.VMEM((3, group, 8, block), F32),
        pltpu.VMEM((3, group, hd + 16, block), F32),
        pltpu.VMEM((3, group, 8, block), F32),
        pltpu.VMEM((group, hd, block), F32),
        pltpu.VMEM((2 * block // 128, 128), F32),
        pltpu.VMEM((2 * kvh, 2 * block // 128, 128), F32),
        pltpu.VMEM((group, hd, block), BF16),
        pltpu.VMEM((group * block, hd), BF16),
        pltpu.VMEM((group, 8, block), F32),
        pltpu.VMEM((3 * block, group * block), BF16),
        pltpu.VMEM((block, hd), F32),
        pltpu.VMEM((block, hd), F32),
        pltpu.VMEM((2, block, hd), BF16),
        pltpu.VMEM((2, block, hd), BF16),
        pltpu.VMEM((2, block, hd), BF16),
        pltpu.VMEM((2, block, hd), BF16),
        pltpu.VMEM((2, block, block), BF16),
        pltpu.VMEM((block, hd), BF16),
        pltpu.VMEM((block, hd), BF16),
        pltpu.VMEM((block, width), BF16),
        pltpu.VMEM((block, width), BF16),
        pltpu.SemaphoreType.DMA((4,)),
        pltpu.SemaphoreType.DMA((4,)),
        pltpu.SemaphoreType.DMA((4,)),
        pltpu.SemaphoreType.DMA((11,)),
        pltpu.SemaphoreType.DMA((11,)),
        pltpu.SemaphoreType.DMA((2,)),
        pltpu.SemaphoreType.DMA((4,)),
        pltpu.SemaphoreType.DMA((4,)),
        pltpu.SemaphoreType.DMA((4,)),
    ]
    wide = jax.ShapeDtypeStruct(query_rows.shape, BF16)
    part = jax.ShapeDtypeStruct(key_rows.shape, F32)
    thin = jax.ShapeDtypeStruct(key_rows.shape, BF16)
    results = pl.pallas_call(
        functools.partial(kernel, blocks, rows, group, kvh),
        out_shape=(wide, wide, part, part, thin, thin),
        in_specs=[pl.BlockSpec(memory_space=pltpu.SMEM)] + [anywhere] * 4,
        out_specs=(anywhere,) * 6,
        scratch_shapes=scratch,
        compiler_params=pltpu.CompilerParams(
            collective_id=0, has_side_effects=True, vmem_limit_bytes=60 * 2**20
        ),
        name="moba",
    )(chosen.T, query_rows, key_rows, value_rows, grad_out)
    return pl.pallas_call(
        finish,
        out_shape=(wide, wide, thin, thin),
        in_specs=[anywhere] * 6,
        out_specs=(anywhere,) * 4,
        scratch_shapes=[
            pltpu.VMEM((2, 1, rows, query_rows.shape[1]), BF16),
            pltpu.VMEM((2, *key_rows.shape), F32),
            pltpu.VMEM((2, *key_rows.shape), BF16),
            pltpu.VMEM((2, *key_rows.shape), BF16),
            pltpu.SemaphoreType.DMA((2, 4)),
            pltpu.SemaphoreType.DMA((2,)),
            pltpu.SemaphoreType.DMA((2,)),
            pltpu.SemaphoreType.DMA((2, 4)),
            pltpu.SemaphoreType.DMA((2,)),
        ],
        name="finish",
    )(*results)


def solution(mesh):
    return jax.shard_map(
        shards,
        mesh=mesh,
        in_specs=(P("ctx", "kvh"), P("ctx", "kvh"), P("ctx", "kvh"), P("ctx", "kvh"), P()),
        out_specs=(P("ctx", "kvh"), P("ctx", "kvh"), P("ctx", "kvh"), P("ctx", "kvh")),
        check_vma=False,
    )
```
